512 devices in a mesh: clu: 32 (over y, x, core), col: 16 (over z).
Axes of the slice: x: 4, y: 4, z: 16, core: 2. Of those that a mesh axis runs over, the one named last changes fastest.
Arguments:
- positions: float32 [16384, 2, 128], P(('clu', 'col')), may hold values from -4 to 4
- tension: float32 [16384, 128], P(('clu', 'col')), may hold values from -6 to 6
- bending: float32 [16384], P(('clu', 'col')), may hold values from 0.3 to 3
- moved_order: int32 [512, 32], P(('clu', 'col')), may hold values from 0 to 31, each once within a row
- move_destination: int32 [12288, 1], P(('clu', 'col')), may hold values from 0 to 31; in each aligned block of 24 rows (0 to 23, 24 to 47, ...) at most 2 rows name the same one
- move_target: int32 [12288], P(('clu', 'col')), may hold values from 0 to 31
- far_range: int32 [16384, 1], P(('clu', 'col')), may hold values from 0 to 15; in each aligned block of 32 rows (0 to 31, 32 to 63, ...) at most 4 rows name the same one
- old_basis: bfloat16 [128, 8192], P(None, 'col'), may hold values from -6 to 6
- source_nodes: bfloat16 [2, 8192], P(None, 'col'), may hold values from -4 to 4
Outputs:
- force: float32 [16384, 2, 128], P(('clu', 'col'))
- near_velocity: float32 [16384, 2, 128], P(('clu', 'col'))
- new_basis: float32 [16384, 64, 2, 128], P(('clu', 'col'))
The draws below stay inside these ranges and needn't reach their ends.
Inputs may be any that keep to these rules, and one draw needn't show every extreme that they name: `moved_order`: each row of a device lists its 32 vesicles once each; the first 24 are the moved ones. `move_destination`: among the 24 rows of one device no cluster is named more than 2 times. `far_range`: among the 32 rows of one device no column range is named more than 4 times.
All inputs are finite; a program needn't handle non-finite values.
Results may differ from the reference program's by a relative error of at most 0.0045.
Values may be sent and summed in bfloat16 or wider, within the bound.
A program may use at most 64 MiB of HBM per device.

```python
import math
import jax
import jax.numpy as jnp
import numpy as np
from jax import lax

NODES = 128
RANK = 64
V_DEV = 32
SRC = 512
MOVE_DEV = 24
CAP = 2
CAPF = 4
VES = 16384
MOVES = 12288
SRC_ALL = 8192
N_CLU = 32
N_COL = 16


def with_ends(entries, stream_key, smallest, high):
    longest = entries.shape.index(max(entries.shape))
    spots = []
    for shift in (0, 1):
        where = [jax.random.randint(jax.random.fold_in(stream_key, axis), (), 0, length) for axis, length in enumerate(entries.shape)]
        where[longest] = (where[longest] + shift) % entries.shape[longest]
        spots.append(tuple(where))
    return entries.at[spots[0]].set(smallest).at[spots[1]].set(high)


def block_levels(rng, dims, pieces, low, largest):
    loudness = 1.0
    for axis_at, blocks in pieces:
        heights = jax.random.uniform(jax.random.fold_in(jax.random.fold_in(rng, 6), axis_at), (blocks,), jnp.float32, low / len(pieces), largest / len(pieces))
        loudness = loudness * jnp.repeat(jnp.exp(heights), dims[axis_at] // blocks).reshape((-1,) + (1,) * (len(dims) - 1 - axis_at))
    return loudness


def deal_out(own_key, own, number, rows, number_of, top, limit, lean):
    ranking = jax.random.permutation(own_key, number_of)
    packed, ordinary = load_shares(number_of, rows * top, limit, lean, True), load_shares(number_of, rows * top, limit, lean, False)
    places = jnp.arange(number_of)

    def named(lengths, rotation):
        used = int((lengths > 0).sum())
        fixed = max(1, used // 4)
        shifted = fixed + (places - fixed + rotation * (used - fixed)) % max(1, number_of - fixed)
        return jnp.zeros((number_of,), jnp.int32).at[ranking[jnp.where(places < fixed, places, shifted)]].set(jnp.asarray(lengths, jnp.int32))

    lengths = jnp.where(number % 4 == 0, named(packed, number // 4), named(ordinary, number - number // 4 - 1))
    mixed = jax.random.permutation(jax.random.fold_in(own, 3), number_of)
    donor, taker = mixed[0:number_of // 2 * 2:2], mixed[1:number_of // 2 * 2:2]
    room = jnp.minimum(lengths[donor] - 1, limit - lengths[taker]) // 2
    room = jnp.where((donor == ranking[0]) | (taker == ranking[0]) | (lengths[taker] == 0), 0, jnp.maximum(room, 0))
    shifted = jax.random.randint(jax.random.fold_in(own, 4), (number_of // 2,), 0, 1 << 20) % (room + 1)
    lengths = lengths.at[donor].add(-shifted).at[taker].add(shifted)
    labels = jnp.searchsorted(jnp.cumsum(lengths), jnp.arange(rows * top), side="right").astype(jnp.int32)
    table = labels.reshape(top, rows).T
    table = table[jax.random.permutation(jax.random.fold_in(own, 1), rows)]
    rotation = jax.random.randint(jax.random.fold_in(own, 2), (rows, 1), 0, top)
    return jnp.take_along_axis(table, (jnp.arange(top)[None, :] + rotation) % top, axis=1)


def load_shares(number_of, total, reach, skew, full):
    weights = [(1 << 20) // math.isqrt(grade ** skew) + 1 for grade in range(1, number_of + 1)]
    largest = reach if full else min(reach, max(-(-total // number_of), total * weights[0] // sum(weights)))
    least = 1 if total - largest >= number_of - 1 else 0
    holding, surplus = [largest] + [least] * (number_of - 1), total - largest - least * (number_of - 1)
    while surplus > 0:
        free = [i for i in range(1, number_of) if holding[i] < largest] or [i for i in range(1, number_of) if holding[i] < reach]
        pool, remaining = sum([weights[i] for i in free]), surplus
        for i in free:
            extra = min(reach - holding[i], max(1, remaining * weights[i] // pool), surplus)
            holding[i] = holding[i] + extra
            surplus = surplus - extra
    return np.array(holding)


def noise(rng, shape, scale, bound, shards=(), held_as=jnp.bfloat16):
    drawn = scale * jax.random.normal(rng, shape, jnp.float32)
    if shards:
        drawn = drawn * block_levels(rng, shape, shards, -0.22, 0.18)
    return jnp.clip(drawn, -bound, bound).astype(held_as)


def setup_inputs(seed: int = 0) -> dict:
    streams_of = jax.random.split(jax.random.key(seed), 10)
    positions = noise(streams_of[0], (VES, 2, NODES), 1.0, 4.0, ((0, 512),), jnp.float32)
    tension = noise(streams_of[1], (VES, NODES), 1.0, 6.0, ((0, 512),), jnp.float32)
    bending = jnp.clip(jnp.exp(math.log(3.0) - 2.3025851 * jax.random.uniform(streams_of[2], (VES,), jnp.float32) ** block_levels(streams_of[2], (VES,), ((0, 512),), -0.2, 0.2)), 0.3, 3.0)
    moved_order = jax.vmap(lambda own: jax.random.permutation(own, V_DEV))(jax.random.split(streams_of[3], (N_CLU * N_COL))).reshape((N_CLU * N_COL, V_DEV)).astype(jnp.int32)
    move_destination_keys = jax.random.split(jax.random.fold_in(streams_of[4], 1), MOVES // MOVE_DEV)
    move_destination_turns = jax.random.permutation(jax.random.fold_in(streams_of[4], 3), MOVES // MOVE_DEV)
    move_destination = jax.vmap(lambda own, number: deal_out(jax.random.fold_in(streams_of[4], 2), own, number, MOVE_DEV, N_CLU, 1, CAP, 2))(move_destination_keys, move_destination_turns).reshape((MOVES, 1))
    move_target = with_ends(jax.random.randint(streams_of[5], (MOVES,), 0, V_DEV), jax.random.fold_in(streams_of[5], 1), 0, V_DEV - 1).astype(jnp.int32)
    far_range_keys = jax.random.split(jax.random.fold_in(streams_of[6], 1), VES // V_DEV)
    far_range_turns = jax.random.permutation(jax.random.fold_in(streams_of[6], 3), VES // V_DEV)
    far_range = jax.vmap(lambda own, number: deal_out(jax.random.fold_in(streams_of[6], 2), own, number, V_DEV, N_COL, 1, CAPF, 2))(far_range_keys, far_range_turns).reshape((VES, 1))
    old_basis = noise(streams_of[7], (2 * RANK, SRC_ALL), 1.0, 6.0, ((1, 16),))
    source_nodes = noise(streams_of[8], (2, SRC_ALL), 1.0, 4.0, ((1, 16),))
    return dict(positions=positions, tension=tension, bending=bending, moved_order=moved_order, move_destination=move_destination, move_target=move_target, far_range=far_range, old_basis=old_basis, source_nodes=source_nodes)


EPS_SQUARED = 0.01

def spectral_tables(node_count):
    half_count = node_count // 2
    node_index = lax.broadcasted_iota(jnp.int32, (node_count, half_count + 1), 0)
    wave_index = lax.broadcasted_iota(jnp.int32, (node_count, half_count + 1), 1)
    phase_angle = (node_index * wave_index % node_count).astype(jnp.float32) * (2.0 * math.pi / node_count)
    cosine_table = jnp.cos(phase_angle)
    sine_table = jnp.sin(phase_angle)
    wavenumber = lax.broadcasted_iota(jnp.int32, (half_count + 1,), 0).astype(jnp.float32)
    inside = jnp.logical_and(wavenumber > 0, wavenumber < half_count)
    first_weight = jnp.where(inside, 2.0 * wavenumber / half_count, 0.0).astype(jnp.float32)
    fourth_weight = jnp.where(inside, 2.0 * (wavenumber / half_count) ** 4, jnp.where(wavenumber == half_count, 1.0, 0.0)).astype(jnp.float32)
    highest = lax.Precision.HIGHEST
    derivative = (jnp.dot(cosine_table * first_weight, sine_table.T, precision=highest) - jnp.dot(sine_table * first_weight, cosine_table.T, precision=highest)) / node_count
    bending_table = (jnp.dot(cosine_table * fourth_weight, cosine_table.T, precision=highest) + jnp.dot(sine_table * fourth_weight, sine_table.T, precision=highest)) / node_count
    return (derivative, bending_table)

def membrane_force(positions, tension, bending, derivative, bending_table):
    vesicles, node_count = (positions.shape[0], positions.shape[2])
    highest = lax.Precision.HIGHEST
    flat_rows = positions.reshape(vesicles * 2, node_count)
    slope = jnp.dot(flat_rows, derivative.T, precision=highest).reshape(vesicles, 2, node_count)
    fourth = jnp.dot(flat_rows, bending_table.T, precision=highest).reshape(vesicles, 2, node_count)
    pulled = (tension[:, None, :] * slope).reshape(vesicles * 2, node_count)
    tension_part = jnp.dot(pulled, derivative.T, precision=highest).reshape(vesicles, 2, node_count)
    return tension_part - bending[:, None, None] * fourth

def near_velocity_block(target_nodes, source_nodes, source_force):
    delta_x = target_nodes[0][:, None] - source_nodes[0][None, :]
    delta_y = target_nodes[1][:, None] - source_nodes[1][None, :]
    spread = delta_x * delta_x + delta_y * delta_y + EPS_SQUARED
    log_part = -0.5 * jnp.log(spread)
    push_x = source_force[0][None, :]
    push_y = source_force[1][None, :]
    along = (delta_x * push_x + delta_y * push_y) / spread
    speed_x = lax.optimization_barrier(jnp.sum(log_part * push_x + delta_x * along, axis=1))
    speed_y = lax.optimization_barrier(jnp.sum(log_part * push_y + delta_y * along, axis=1))
    return jnp.stack([speed_x, speed_y]) / target_nodes.shape[1]

def far_kernel(targets, sources):
    delta_x = targets[..., 0, None, :] - sources[..., 0, :, None]
    delta_y = targets[..., 1, None, :] - sources[..., 1, :, None]
    spread = delta_x * delta_x + delta_y * delta_y + EPS_SQUARED
    log_part = -0.5 * jnp.log(spread)
    first_first = log_part + delta_x * delta_x / spread
    first_second = delta_x * delta_y / spread
    second_second = log_part + delta_y * delta_y / spread
    upper_rows = jnp.stack([first_first, first_second], axis=-3)
    lower_rows = jnp.stack([first_second, second_second], axis=-3)
    return jnp.stack([upper_rows, lower_rows], axis=-4).astype(jnp.bfloat16)

def reference(positions, tension, bending, moved_order, move_destination, move_target, far_range, old_basis, source_nodes):
    highest = lax.Precision.HIGHEST
    derivative, bending_table = spectral_tables(NODES)
    force = membrane_force(positions, tension, bending, derivative, bending_table)
    move_ids = jnp.arange(MOVES, dtype=jnp.int32)
    device_ids = move_ids // MOVE_DEV
    within = move_ids % MOVE_DEV
    source_ves = device_ids * V_DEV + moved_order[device_ids, within].astype(jnp.int32)
    target_ves = (move_destination[:, 0].astype(jnp.int32) * N_COL + device_ids % N_COL) * V_DEV + move_target.astype(jnp.int32)

    def near_rows(which):
        sources = lax.dynamic_slice_in_dim(source_ves, which * MOVE_DEV, MOVE_DEV, 0)
        targets = lax.dynamic_slice_in_dim(target_ves, which * MOVE_DEV, MOVE_DEV, 0)
        return jax.vmap(near_velocity_block)(positions[targets], positions[sources], force[sources])
    speeds = lax.map(near_rows, jnp.arange(MOVES // MOVE_DEV, dtype=jnp.int32)).reshape(MOVES, 2, NODES)
    near_velocity = jnp.zeros((VES, 2, NODES), jnp.float32).at[target_ves].add(speeds)
    chosen_all = far_range[:, 0].astype(jnp.int32)

    def far_rows(which):
        rows = lax.dynamic_slice_in_dim(positions, which * V_DEV, V_DEV, 0)
        chosen = lax.dynamic_slice_in_dim(chosen_all, which * V_DEV, V_DEV, 0)

        def take_range(index):
            start = (index * SRC).astype(jnp.int32)
            return (lax.dynamic_slice_in_dim(old_basis, start, SRC, 1), lax.dynamic_slice_in_dim(source_nodes, start, SRC, 1))
        basis_rows, source_rows = jax.vmap(take_range)(chosen)
        kernel = far_kernel(rows, source_rows.astype(jnp.float32))
        stacked = basis_rows.reshape(V_DEV, 2, RANK, SRC).astype(jnp.float32)
        return jnp.einsum('geks,gedsn->gkdn', stacked, kernel.astype(jnp.float32), precision=highest)
    sketch = lax.map(far_rows, jnp.arange(VES // V_DEV, dtype=jnp.int32)).reshape(VES, RANK, 2 * NODES)
    gram = jnp.einsum('vkm,vjm->kj', sketch, sketch, precision=highest)
    lower_factor = jnp.linalg.cholesky(gram)
    lower_inverse = jax.scipy.linalg.solve_triangular(lower_factor, jnp.eye(RANK, dtype=jnp.float32), lower=True)
    scale_factor = math.sqrt(2.0 * NODES * VES)
    new_basis = jnp.einsum('kj,vjm->vkm', lower_inverse, sketch, precision=highest).reshape(VES, RANK, 2, NODES) * scale_factor
    return (force, near_velocity, new_basis)
```

```python
import functools
import math

import jax
import jax.numpy as jnp
import numpy as np
from jax import lax
from jax.experimental import pallas as pl
from jax.experimental.pallas import tpu as pltpu
from jax.sharding import PartitionSpec as P

EPS_SQUARED = 0.01
HIGHEST = lax.Precision.HIGHEST
MESH = pl.DeviceIdType.MESH
SUB = 2


def spectral_tables(node_count):
    half_count = node_count // 2
    node_index = np.arange(node_count)[:, None]
    wave_index = np.arange(half_count + 1)[None, :]
    phase_angle = (node_index * wave_index % node_count) * (2.0 * math.pi / node_count)
    cosine_table = np.cos(phase_angle)
    sine_table = np.sin(phase_angle)
    wavenumber = np.arange(half_count + 1).astype(np.float64)
    inside = (wavenumber > 0) & (wavenumber < half_count)
    first_weight = np.where(inside, 2.0 * wavenumber / half_count, 0.0)
    fourth_weight = np.where(
        inside, 2.0 * (wavenumber / half_count) ** 4, np.where(wavenumber == half_count, 1.0, 0.0)
    )
    derivative = (
        (cosine_table * first_weight) @ sine_table.T - (sine_table * first_weight) @ cosine_table.T
    ) / node_count
    bending_table = (
        (cosine_table * fourth_weight) @ cosine_table.T
        + (sine_table * fourth_weight) @ sine_table.T
    ) / node_count
    return np.concatenate([derivative.T, bending_table.T], axis=1).astype(np.float32)


def iota(shape, dim):
    return lax.broadcasted_iota(jnp.int32, shape, dim)


def main_kernel(
    sizes,
    far_ref,
    table_ref,
    pos_ref,
    tension_ref,
    bending_ref,
    order_ref,
    dest_ref,
    goal_ref,
    basis_ref,
    nodes_ref,
    force_ref,
    near_ref,
    sketch_ref,
    gram_ref,
    move_out,
    move_in,
    goal_nodes,
    speeds,
    all_basis,
    all_nodes,
    kernels,
    sketch,
    part_out,
    part_in,
    ring_out,
    ring_in,
    sum_row,
    move_send,
    move_recv,
    node_send,
    node_recv,
    ring_send,
    ring_recv,
    pair_send,
    pair_recv,
    own_sem,
    part_send,
    part_recv,
    line_send,
    line_recv,
    full_send,
    full_recv,
    sketch_sem,
):
    n_clu, n_col, vesicles, node_count, move_count, rank_count, source_count = sizes
    me = lax.axis_index("clu")
    z = lax.axis_index("col")
    core = lax.rem(me, 2)
    partner = me + 1 - 2 * core
    up = {"col": lax.rem(z + 1, n_col)}
    down = {"col": lax.rem(z + n_col - 1, n_col)}
    plus_steps = n_col // 2
    minus_steps = n_col - 1 - plus_steps
    sub_rows = rank_count // SUB

    barrier = pltpu.get_barrier_semaphore()

    @pl.loop(1, n_clu)
    def _(k):
        pl.semaphore_signal(
            barrier, inc=1, device_id={"clu": lax.rem(me + k, n_clu)}, device_id_type=MESH
        )

    @pl.loop(1, n_col)
    def _(k):
        pl.semaphore_signal(
            barrier, inc=1, device_id={"col": lax.rem(z + k, n_col)}, device_id_type=MESH
        )

    pl.semaphore_wait(barrier, n_clu + n_col - 2)

    def node_copy(k):
        return pltpu.make_async_remote_copy(
            src_ref=nodes_ref,
            dst_ref=all_nodes.at[z],
            send_sem=node_send.at[k],
            recv_sem=node_recv.at[k],
            device_id={"col": lax.rem(z + k, n_col)},
            device_id_type=MESH,
        )

    @pl.loop(1, n_col)
    def _(k):
        node_copy(k).start()

    def ring_copy(way, step, sub):
        origin = lax.rem(z + n_col - step, n_col) if way == 0 else lax.rem(z + step, n_col)
        rows = pl.ds(sub * sub_rows, sub_rows)
        source = (
            basis_ref.at[core, rows] if step == 0 else all_basis.at[origin, core, rows]
        )
        return pltpu.make_async_remote_copy(
            src_ref=source,
            dst_ref=all_basis.at[origin, core, rows],
            send_sem=ring_send.at[way, step, sub],
            recv_sem=ring_recv.at[way, step, sub],
            device_id=up if way == 0 else down,
            device_id_type=MESH,
        )

    def ring_wait(way, step, sub):
        origin = (
            lax.rem(z + n_col - step - 1, n_col) if way == 0 else lax.rem(z + step + 1, n_col)
        )
        rows = pl.ds(sub * sub_rows, sub_rows)
        pltpu.make_async_remote_copy(
            src_ref=all_basis.at[origin, core, rows],
            dst_ref=all_basis.at[origin, core, rows],
            send_sem=ring_send.at[way, step, sub],
            recv_sem=ring_recv.at[way, step, sub],
            device_id=up if way == 0 else down,
            device_id_type=MESH,
        ).wait_recv()

    def pair_copy(offset, half):
        origin = lax.rem(z + offset, n_col)
        return pltpu.make_async_remote_copy(
            src_ref=all_basis.at[origin, half],
            dst_ref=all_basis.at[origin, half],
            send_sem=pair_send.at[offset],
            recv_sem=pair_recv.at[lax.rem(z + offset, n_col)],
            device_id={"clu": partner},
            device_id_type=MESH,
        )

    def ring_service(step):
        for way, count in ((0, plus_steps), (1, minus_steps)):
            if step < count:
                for sub in range(SUB):
                    ring_wait(way, step, sub)
                    if step + 1 < count:
                        ring_copy(way, step + 1, sub).start()
                offset = n_col - step - 1 if way == 0 else step + 1
                pair_copy(offset, core).start()

    for sub in range(SUB):
        ring_copy(0, 0, sub).start()
        ring_copy(1, 0, sub).start()
    own_basis = pltpu.make_async_copy(basis_ref, all_basis.at[z], own_sem.at[0])
    own_basis.start()
    own_nodes = pltpu.make_async_copy(nodes_ref, all_nodes.at[z], own_sem.at[1])
    own_nodes.start()

    rows_x = pl.ds(0, vesicles, stride=2)
    rows_y = pl.ds(1, vesicles, stride=2)
    flat = jnp.concatenate([pos_ref[rows_x, :], pos_ref[rows_y, :]], axis=0)
    table = table_ref[...]
    both = jnp.dot(flat, table, precision=HIGHEST, preferred_element_type=jnp.float32)
    slope = both[:, :node_count]
    fourth = both[:, node_count:]
    tension = tension_ref[...]
    pulled = slope * jnp.concatenate([tension, tension], axis=0)
    stretch = jnp.dot(
        pulled, table[:, :node_count], precision=HIGHEST, preferred_element_type=jnp.float32
    )
    square = (vesicles, vesicles)
    bending = jnp.sum(
        jnp.where(iota(square, 0) == iota(square, 1), bending_ref[...], 0.0), axis=1, keepdims=True
    )
    force = stretch - jnp.concatenate([bending, bending], axis=0) * fourth
    force_ref[rows_x, :] = force[:vesicles]
    force_ref[rows_y, :] = force[vesicles:]
    carried = jnp.concatenate([flat, force], axis=0)

    pairs = (move_count, move_count)
    dest_col = dest_ref[...].astype(jnp.float32)
    dest_row = jnp.sum(
        jnp.where(iota(pairs, 0) == iota(pairs, 1), dest_col, 0.0), axis=0, keepdims=True
    )
    earlier = jnp.sum(
        jnp.where((dest_col == dest_row) & (iota(pairs, 0) < iota(pairs, 1)), 1.0, 0.0),
        axis=0,
        keepdims=True,
    )
    slot_rows = n_clu * 8
    wide = (slot_rows, move_count)
    match = (dest_row == (iota(wide, 0) // 8).astype(jnp.float32)) & (
        earlier == (iota(wide, 0) // 4 % 2).astype(jnp.float32)
    )
    order_row = order_ref[:, :move_count].astype(jnp.float32)
    goal_row = goal_ref[...].astype(jnp.float32) + 1.0
    found = jnp.sum(jnp.where(match, 1.0, 0.0), axis=1, keepdims=True)
    chosen = jnp.sum(jnp.where(match, order_row, 0.0), axis=1, keepdims=True)
    goal = jnp.sum(jnp.where(match, goal_row, 0.0), axis=1, keepdims=True)
    table_shape = (slot_rows, 4 * vesicles)
    part_first = (iota(table_shape, 0) % 4 * vesicles).astype(jnp.float32)
    lane = iota(table_shape, 1).astype(jnp.float32)
    pack = jnp.where((lane == part_first + chosen) & (found > 0.0), 1.0, 0.0)
    packed = jnp.dot(pack, carried, precision=HIGHEST, preferred_element_type=jnp.float32)
    move_out[:, 0] = packed.reshape(n_clu, 8, node_count)
    move_out[:, 1] = jnp.broadcast_to(goal, (slot_rows, node_count)).reshape(n_clu, 8, node_count)

    def move_copy(k):
        other = lax.rem(me + k, n_clu)
        return pltpu.make_async_remote_copy(
            src_ref=move_out.at[other],
            dst_ref=move_in.at[me],
            send_sem=move_send.at[k],
            recv_sem=move_recv.at[k],
            device_id={"clu": other},
            device_id_type=MESH,
        )

    def from_peer(buffer, sems_out, sems_in, axis, k, count, index):
        other = lax.rem(index + count - k, count)
        return pltpu.make_async_remote_copy(
            src_ref=buffer.at[other],
            dst_ref=buffer.at[other],
            send_sem=sems_out.at[k],
            recv_sem=sems_in.at[k],
            device_id={axis: other},
            device_id_type=MESH,
        )

    @pl.loop(1, n_clu)
    def _(k):
        move_copy(k).start()

    own_move = pltpu.make_async_copy(move_out.at[me], move_in.at[me], own_sem.at[2])
    own_move.start()

    ring_service(0)
    own_nodes.wait()

    @pl.loop(1, n_col)
    def _(k):
        from_peer(all_nodes, node_send, node_recv, "col", k, n_col, z).wait_recv()

    chunk = 128

    def form_kernel(b):
        nodes = all_nodes[far_ref[b]]
        target_x = pos_ref[pl.ds(2 * b, 1), :]
        target_y = pos_ref[pl.ds(2 * b + 1, 1), :]
        for part in range(source_count // chunk):
            piece = nodes[:, part * chunk : (part + 1) * chunk]
            turned = jnp.concatenate([piece] * 4, axis=0).T
            delta_x = target_x - turned[:, 0:1]
            delta_y = target_y - turned[:, 1:2]
            square_x = delta_x * delta_x
            square_y = delta_y * delta_y
            spread = square_x + square_y + EPS_SQUARED
            log_part = -0.5 * jnp.log(spread)
            inverse = 1.0 / spread
            rows = pl.ds(part * chunk, chunk)
            kernels[b, rows, 0:node_count] = (log_part + square_x * inverse).astype(jnp.bfloat16)
            kernels[b, rows, node_count : 2 * node_count] = (
                delta_x * delta_y * inverse
            ).astype(jnp.bfloat16)
            kernels[b, rows, 2 * node_count : 3 * node_count] = (
                log_part + square_y * inverse
            ).astype(jnp.bfloat16)

    segments = max(plus_steps, 1)
    each = -(-vesicles // segments)
    for segment in range(segments):
        if segment > 0:
            ring_service(segment)

        @pl.loop(segment * each, min((segment + 1) * each, vesicles))
        def _(b):
            form_kernel(b)

    own_basis.wait()

    @pl.loop(1, n_col)
    def _(k):
        pair_copy(k, 1 - core).wait_recv()

    gram_shape = (2 * rank_count, 2 * rank_count)

    def sketch_row(b, total):
        basis = all_basis[far_ref[b]].reshape(2 * rank_count, source_count)
        product = jnp.dot(basis, kernels[b], preferred_element_type=jnp.float32)
        first = product[:rank_count]
        second = product[rank_count:]
        row = first[:, : 2 * node_count] + second[:, node_count:]
        sketch[b] = row
        high = row.astype(jnp.bfloat16)
        low = (row - high.astype(jnp.float32)).astype(jnp.bfloat16)
        stacked = jnp.concatenate([high, low], axis=0)
        return total + lax.dot_general(
            stacked, stacked, (((1,), (1,)), ((), ())), preferred_element_type=jnp.float32
        )

    total = lax.fori_loop(0, vesicles, sketch_row, jnp.zeros(gram_shape, jnp.float32))
    keep_sketch = pltpu.make_async_copy(sketch, sketch_ref, sketch_sem)
    keep_sketch.start()
    gram = (
        total[:rank_count, :rank_count]
        + total[:rank_count, rank_count:]
        + total[rank_count:, :rank_count]
        + total[rank_count:, rank_count:]
    )
    half = rank_count // 2
    folded = jnp.concatenate([gram[:half], gram[half:]], axis=1)
    own_rows = half // n_clu
    for row in range(half):
        part_out[row // own_rows, row % own_rows : row % own_rows + 1, :] = folded[row : row + 1]

    def part_copy(k):
        other = lax.rem(me + k, n_clu)
        return pltpu.make_async_remote_copy(
            src_ref=part_out.at[other],
            dst_ref=part_in.at[me],
            send_sem=part_send.at[k],
            recv_sem=part_recv.at[k],
            device_id={"clu": other},
            device_id_type=MESH,
        )

    @pl.loop(1, n_clu)
    def _(k):
        part_copy(k).start()

    own_move.wait()

    @pl.loop(1, n_clu)
    def _(k):
        from_peer(move_in, move_send, move_recv, "clu", k, n_clu, me).wait_recv()

    goals = move_in[:, 1].reshape(slot_rows, node_count)
    goal_shape = (slot_rows, 2 * vesicles)
    part_index = iota(goal_shape, 0) % 4
    goal_lane = iota(goal_shape, 1).astype(jnp.float32)
    goal_value = goals[:, : 2 * vesicles]
    goal_hot = jnp.where(
        (goal_lane == (part_index * vesicles - 1).astype(jnp.float32) + goal_value)
        & (part_index < 2)
        & (goal_value > 0.0),
        1.0,
        0.0,
    )
    goal_nodes[...] = jnp.dot(
        goal_hot, flat, precision=HIGHEST, preferred_element_type=jnp.float32
    ).reshape(n_clu, 8, node_count)

    def near_pair(src):
        turned = move_in[src, 0].T
        goal_tile = goal_nodes[src]
        results = []
        for slot in range(2):
            first = 4 * slot
            delta_x = goal_tile[first : first + 1] - turned[:, first : first + 1]
            delta_y = goal_tile[first + 1 : first + 2] - turned[:, first + 1 : first + 2]
            push_x = turned[:, first + 2 : first + 3]
            push_y = turned[:, first + 3 : first + 4]
            spread = delta_x * delta_x + delta_y * delta_y + EPS_SQUARED
            log_part = -0.5 * jnp.log(spread)
            along = (delta_x * push_x + delta_y * push_y) / spread
            results.append(jnp.sum(log_part * push_x + delta_x * along, axis=0, keepdims=True))
            results.append(jnp.sum(log_part * push_y + delta_y * along, axis=0, keepdims=True))
            results.append(jnp.zeros((2, node_count), jnp.float32))
        speeds[src] = jnp.concatenate(results, axis=0)

    @pl.loop(0, n_clu // 2)
    def _(src):
        near_pair(src)

    part_in[me] = part_out[me]

    @pl.loop(1, n_clu)
    def _(k):
        from_peer(part_in, part_send, part_recv, "clu", k, n_clu, me).wait_recv()

    ring_out[...] = jnp.sum(part_in[...], axis=0)

    def line_copy(k):
        return pltpu.make_async_remote_copy(
            src_ref=ring_out,
            dst_ref=ring_in.at[z],
            send_sem=line_send.at[k],
            recv_sem=line_recv.at[k],
            device_id={"col": lax.rem(z + k, n_col)},
            device_id_type=MESH,
        )

    @pl.loop(1, n_col)
    def _(k):
        line_copy(k).start()

    @pl.loop(n_clu // 2, n_clu)
    def _(src):
        near_pair(src)

    ring_in[z] = ring_out[...]

    @pl.loop(1, n_col)
    def _(k):
        from_peer(ring_in, line_send, line_recv, "col", k, n_col, z).wait_recv()

    sum_row[...] = jnp.sum(ring_in[...], axis=0)

    def full_copy(k):
        return pltpu.make_async_remote_copy(
            src_ref=sum_row,
            dst_ref=gram_ref.at[me],
            send_sem=full_send.at[k],
            recv_sem=full_recv.at[k],
            device_id={"clu": lax.rem(me + k, n_clu)},
            device_id_type=MESH,
        )

    @pl.loop(1, n_clu)
    def _(k):
        full_copy(k).start()

    gram_ref[me] = sum_row[...]
    near = lax.dot_general(
        goal_hot,
        speeds[...].reshape(slot_rows, node_count),
        (((0,), (0,)), ((), ())),
        precision=HIGHEST,
        preferred_element_type=jnp.float32,
    ) * (1.0 / node_count)
    near_ref[rows_x, :] = near[:vesicles]
    near_ref[rows_y, :] = near[vesicles:]

    for step in range(plus_steps):
        for way, count in ((0, plus_steps), (1, minus_steps)):
            if step < count:
                for sub in range(SUB):
                    ring_copy(way, step, sub).wait_send()

    @pl.loop(1, n_col)
    def _(k):
        node_copy(k).wait_send()
        line_copy(k).wait_send()
        pair_copy(k, core).wait_send()

    keep_sketch.wait()

    @pl.loop(1, n_clu)
    def _(k):
        move_copy(k).wait_send()
        part_copy(k).wait_send()
        full_copy(k).wait_send()
        from_peer(gram_ref, full_send, full_recv, "clu", k, n_clu, me).wait_recv()


def finish_kernel(
    scale_factor, gram_ref, sketch_ref, force_in, near_in, basis_out, force_out, near_out, inverse
):
    rank_count = sketch_ref.shape[1]
    node_count = sketch_ref.shape[2] // 2

    @pl.when(pl.program_id(0) == 0)
    def _():
        force_out[...] = force_in[...]
        near_out[...] = near_in[...]
        folded = gram_ref[...]
        gram = jnp.concatenate([folded[:, :rank_count], folded[:, rank_count:]], axis=0)
        square = (rank_count, rank_count)
        eye = jnp.where(iota(square, 0) == iota(square, 1), 1.0, 0.0)
        joined = jnp.concatenate([gram, eye], axis=1)
        tiles = [joined[8 * t : 8 * t + 8] for t in range(rank_count // 8)]
        below = iota((8, 1), 0)
        for j in range(rank_count):
            home, spot = divmod(j, 8)
            pivot_row = tiles[home][spot : spot + 1]
            scaled = pivot_row / pivot_row[:, j : j + 1]
            for t in range(home, rank_count // 8):
                factor = tiles[t][:, j : j + 1]
                if t == home:
                    factor = jnp.where(below > spot, factor, 0.0)
                tiles[t] = tiles[t] - factor * scaled
        whole = jnp.concatenate(tiles, axis=0)
        pivots = jnp.sum(whole[:, :rank_count] * eye, axis=1, keepdims=True)
        inverse[...] = whole[:, rank_count:] * (scale_factor / jnp.sqrt(pivots))

    lower = inverse[...]
    for b in range(sketch_ref.shape[0]):
        result = jnp.dot(
            lower, sketch_ref[b], precision=HIGHEST, preferred_element_type=jnp.float32
        )
        basis_out[b, pl.ds(0, rank_count, stride=2), :] = result[:, :node_count]
        basis_out[b, pl.ds(1, rank_count, stride=2), :] = result[:, node_count:]


def per_device(
    positions,
    tension,
    bending,
    moved_order,
    move_destination,
    move_target,
    far_range,
    old_basis,
    source_nodes,
):
    n_clu, n_col = lax.axis_size("clu"), lax.axis_size("col")
    vesicles, node_count = positions.shape[0], positions.shape[2]
    move_count = move_target.shape[0]
    rank_count, source_count = old_basis.shape[0] // 2, old_basis.shape[1]
    half = rank_count // 2
    own_rows = half // n_clu
    plus_steps = n_col // 2
    f32, bf16 = jnp.float32, jnp.bfloat16
    vmem, dma = pltpu.VMEM, pltpu.SemaphoreType.DMA
    in_vmem = pl.BlockSpec(memory_space=pltpu.VMEM)
    sizes = (n_clu, n_col, vesicles, node_count, move_count, rank_count, source_count)
    force, near, sketch, gram = pl.pallas_call(
        functools.partial(main_kernel, sizes),
        out_shape=(
            jax.ShapeDtypeStruct((2 * vesicles, node_count), f32),
            jax.ShapeDtypeStruct((2 * vesicles, node_count), f32),
            jax.ShapeDtypeStruct((vesicles, rank_count, 2 * node_count), f32),
            jax.ShapeDtypeStruct((n_clu, own_rows, 2 * rank_count), f32),
        ),
        in_specs=[pl.BlockSpec(memory_space=pltpu.SMEM)] + [in_vmem] * 9,
        out_specs=(in_vmem, in_vmem, pl.BlockSpec(memory_space=pl.ANY), in_vmem),
        scratch_shapes=[
            vmem((n_clu, 2, 8, node_count), f32),
            vmem((n_clu, 2, 8, node_count), f32),
            vmem((n_clu, 8, node_count), f32),
            vmem((n_clu, 8, node_count), f32),
            vmem((n_col, 2, rank_count, source_count), bf16),
            vmem((n_col, 2, source_count), f32),
            vmem((vesicles, source_count, 3 * node_count), bf16),
            vmem((vesicles, rank_count, 2 * node_count), f32),
            vmem((n_clu, own_rows, 2 * rank_count), f32),
            vmem((n_clu, own_rows, 2 * rank_count), f32),
            vmem((own_rows, 2 * rank_count), f32),
            vmem((n_col, own_rows, 2 * rank_count), f32),
            vmem((own_rows, 2 * rank_count), f32),
            dma((n_clu,)),
            dma((n_clu,)),
            dma((n_col,)),
            dma((n_col,)),
            dma((2, plus_steps, SUB)),
            dma((2, plus_steps, SUB)),
            dma((n_col,)),
            dma((n_col,)),
            dma((3,)),
            dma((n_clu,)),
            dma((n_clu,)),
            dma((n_col,)),
            dma((n_col,)),
            dma((n_clu,)),
            dma((n_clu,)),
            dma,
        ],
        compiler_params=pltpu.CompilerParams(
            collective_id=0, has_side_effects=True, vmem_limit_bytes=48 * 1024 * 1024
        ),
        name="main_step",
    )(
        far_range.reshape(vesicles),
        jnp.asarray(spectral_tables(node_count)),
        positions.reshape(2 * vesicles, node_count),
        tension,
        bending.reshape(1, vesicles),
        moved_order,
        move_destination,
        move_target.reshape(1, move_count),
        old_basis.reshape(2, rank_count, source_count),
        source_nodes.astype(f32),
    )
    scale_factor = math.sqrt(2.0 * node_count * vesicles * n_clu * n_col)
    group = 4
    flat_spec = pl.BlockSpec((2 * vesicles, node_count), lambda i: (0, 0))
    new_basis, force, near = pl.pallas_call(
        functools.partial(finish_kernel, scale_factor),
        out_shape=(
            jax.ShapeDtypeStruct((vesicles, 2 * rank_count, node_count), f32),
            jax.ShapeDtypeStruct((2 * vesicles, node_count), f32),
            jax.ShapeDtypeStruct((2 * vesicles, node_count), f32),
        ),
        grid=(vesicles // group,),
        in_specs=[
            pl.BlockSpec((half, 2 * rank_count), lambda i: (0, 0)),
            pl.BlockSpec((group, rank_count, 2 * node_count), lambda i: (i, 0, 0)),
            flat_spec,
            flat_spec,
        ],
        out_specs=(
            pl.BlockSpec((group, 2 * rank_count, node_count), lambda i: (i, 0, 0)),
            flat_spec,
            flat_spec,
        ),
        scratch_shapes=[vmem((rank_count, rank_count), f32)],
        name="finish_step",
    )(gram.reshape(half, 2 * rank_count), sketch, force, near)
    return (
        force.reshape(vesicles, 2, node_count),
        near.reshape(vesicles, 2, node_count),
        new_basis.reshape(vesicles, rank_count, 2, node_count),
    )


def solution(mesh):
    placed = (
        P(("clu", "col"), None, None),
        P(("clu", "col"), None),
        P(("clu", "col")),
        P(("clu", "col"), None),
        P(("clu", "col"), None),
        P(("clu", "col")),
        P(("clu", "col"), None),
        P(None, "col"),
        P(None, "col"),
    )
    return jax.shard_map(
        per_device,
        mesh=mesh,
        in_specs=placed,
        out_specs=(
            P(("clu", "col"), None, None),
            P(("clu", "col"), None, None),
            P(("clu", "col"), None, None, None),
        ),
        check_vma=False,
    )
```

```python
import functools
import math

import jax
import jax.numpy as jnp
import numpy as np
from jax import lax
from jax.experimental import pallas as pl
from jax.experimental.pallas import tpu as pltpu
from jax.sharding import PartitionSpec as P

EPS_SQUARED = 0.01
HIGHEST = lax.Precision.HIGHEST
MESH = pl.DeviceIdType.MESH
SUB = 4
ROWS = 8
VMEM_ALL = 67043328


def spectral_tables(node_count):
    half_count = node_count // 2
    node_index = np.arange(node_count)[:, None]
    wave_index = np.arange(half_count + 1)[None, :]
    phase_angle = (node_index * wave_index % node_count) * (2.0 * math.pi / node_count)
    cosine_table = np.cos(phase_angle)
    sine_table = np.sin(phase_angle)
    wavenumber = np.arange(half_count + 1).astype(np.float64)
    inside = (wavenumber > 0) & (wavenumber < half_count)
    first_weight = np.where(inside, 2.0 * wavenumber / half_count, 0.0)
    fourth_weight = np.where(
        inside, 2.0 * (wavenumber / half_count) ** 4, np.where(wavenumber == half_count, 1.0, 0.0)
    )
    derivative = (
        (cosine_table * first_weight) @ sine_table.T - (sine_table * first_weight) @ cosine_table.T
    ) / node_count
    bending_table = (
        (cosine_table * fourth_weight) @ cosine_table.T
        + (sine_table * fourth_weight) @ sine_table.T
    ) / node_count
    return np.concatenate([derivative.T, bending_table.T], axis=1).astype(np.float32)


def iota(shape, dim):
    return lax.broadcasted_iota(jnp.int32, shape, dim)


def main_kernel(
    sizes,
    far_hbm,
    table_hbm,
    pos_hbm,
    tension_hbm,
    bending_hbm,
    order_hbm,
    dest_hbm,
    goal_hbm,
    basis_ref,
    nodes_ref,
    force_out,
    near_out,
    split_out,
    gram_out,
    force_ref,
    near_ref,
    split_ref,
    gram_ref,
    far_ref,
    table_ref,
    pos_ref,
    tension_ref,
    bending_ref,
    order_ref,
    dest_ref,
    goal_ref,
    move_out,
    move_in,
    goal_nodes,
    speeds,
    all_basis,
    all_nodes,
    wide_nodes,
    kernels,
    part_out,
    part_in,
    line_out,
    line_in,
    sum_row,
    move_send,
    move_recv,
    node_send,
    node_recv,
    ring_send,
    ring_recv,
    pair_send,
    pair_recv,
    own_sem,
    part_send,
    part_recv,
    line_send,
    line_recv,
    full_send,
    full_recv,
):
    n_clu, n_col, vesicles, node_count, move_count, rank_count, source_count = sizes
    me = lax.axis_index("clu")
    z = lax.axis_index("col")
    core = lax.rem(me, 2)
    partner = me + 1 - 2 * core
    up = {"col": lax.rem(z + 1, n_col)}
    down = {"col": lax.rem(z + n_col - 1, n_col)}
    plus_steps = n_col // 2
    minus_steps = n_col - 1 - plus_steps
    sub_rows = rank_count // SUB

    barrier = pltpu.get_barrier_semaphore()

    @pl.loop(1, n_col)
    def _(k):
        pl.semaphore_signal(
            barrier, inc=1, device_id={"col": lax.rem(z + k, n_col)}, device_id_type=MESH
        )

    @pl.loop(1, n_clu)
    def _(k):
        pl.semaphore_signal(
            barrier, inc=1, device_id={"clu": lax.rem(me + k, n_clu)}, device_id_type=MESH
        )

    loads = [
        pltpu.make_async_copy(source, place, own_sem.at[3 + at])
        for at, (source, place) in enumerate(
            (
                (pos_hbm, pos_ref),
                (table_hbm, table_ref),
                (tension_hbm, tension_ref),
                (bending_hbm, bending_ref),
                (order_hbm, order_ref),
                (dest_hbm, dest_ref),
                (goal_hbm, goal_ref),
                (far_hbm, far_ref),
            )
        )
    ]
    for load in loads:
        load.start()
    keeps = [
        pltpu.make_async_copy(source, place, own_sem.at[11 + at])
        for at, (source, place) in enumerate(
            (
                (force_ref, force_out),
                (near_ref, near_out),
                (split_ref, split_out),
                (gram_ref, gram_out),
            )
        )
    ]
    own_basis = pltpu.make_async_copy(basis_ref, all_basis.at[z], own_sem.at[0])
    own_basis.start()
    own_nodes = pltpu.make_async_copy(nodes_ref, all_nodes.at[z], own_sem.at[1])
    own_nodes.start()
    for load in loads:
        load.wait()

    rows_x = pl.ds(0, vesicles, stride=2)
    rows_y = pl.ds(1, vesicles, stride=2)
    flat = jnp.concatenate([pos_ref[rows_x, :], pos_ref[rows_y, :]], axis=0)
    table = table_ref[...]
    both = jnp.dot(flat, table, precision=HIGHEST, preferred_element_type=jnp.float32)
    slope = both[:, :node_count]
    fourth = both[:, node_count:]
    tension = tension_ref[...]
    pulled = slope * jnp.concatenate([tension, tension], axis=0)
    stretch = jnp.dot(
        pulled, table[:, :node_count], precision=HIGHEST, preferred_element_type=jnp.float32
    )
    square = (vesicles, vesicles)
    bending = jnp.sum(
        jnp.where(iota(square, 0) == iota(square, 1), bending_ref[...], 0.0), axis=1, keepdims=True
    )
    force = stretch - jnp.concatenate([bending, bending], axis=0) * fourth
    force_ref[rows_x, :] = force[:vesicles]
    force_ref[rows_y, :] = force[vesicles:]
    keeps[0].start()
    carried = jnp.concatenate([flat, force], axis=0)

    pairs = (move_count, move_count)
    dest_row = dest_ref[...].astype(jnp.float32)
    dest_col = jnp.sum(
        jnp.where(iota(pairs, 0) == iota(pairs, 1), dest_row, 0.0), axis=1, keepdims=True
    )
    earlier = jnp.sum(
        jnp.where((dest_col == dest_row) & (iota(pairs, 0) < iota(pairs, 1)), 1.0, 0.0),
        axis=0,
        keepdims=True,
    )
    slot_rows = n_clu * 8
    wide = (slot_rows, move_count)
    match = (dest_row == (iota(wide, 0) // 8).astype(jnp.float32)) & (
        earlier == (iota(wide, 0) // 4 % 2).astype(jnp.float32)
    )
    order_row = order_ref[:, :move_count].astype(jnp.float32)
    goal_row = goal_ref[...].astype(jnp.float32) + 1.0
    found = jnp.sum(jnp.where(match, 1.0, 0.0), axis=1, keepdims=True)
    chosen = jnp.sum(jnp.where(match, order_row, 0.0), axis=1, keepdims=True)
    goal = jnp.sum(jnp.where(match, goal_row, 0.0), axis=1, keepdims=True)
    table_shape = (slot_rows, 4 * vesicles)
    part_first = (iota(table_shape, 0) % 4 * vesicles).astype(jnp.float32)
    lane = iota(table_shape, 1).astype(jnp.float32)
    pack = jnp.where((lane == part_first + chosen) & (found > 0.0), 1.0, 0.0)
    packed = jnp.dot(pack, carried, precision=HIGHEST, preferred_element_type=jnp.float32)
    move_out[:, 0] = packed.reshape(n_clu, 8, node_count)
    move_out[:, 1] = jnp.broadcast_to(goal, (slot_rows, node_count)).reshape(n_clu, 8, node_count)

    def node_copy(k):
        return pltpu.make_async_remote_copy(
            src_ref=nodes_ref,
            dst_ref=all_nodes.at[z],
            send_sem=node_send.at[k],
            recv_sem=node_recv.at[k],
            device_id={"col": lax.rem(z + k, n_col)},
            device_id_type=MESH,
        )

    def ring_copy(way, step, sub, source):
        origin = lax.rem(z + n_col - step, n_col) if way == 0 else lax.rem(z + step, n_col)
        rows = pl.ds(pl.multiple_of(sub * sub_rows, sub_rows), sub_rows)
        return pltpu.make_async_remote_copy(
            src_ref=all_basis.at[origin, core, rows] if source is None else source.at[core, rows],
            dst_ref=all_basis.at[origin, core, rows],
            send_sem=ring_send.at[way, step, sub],
            recv_sem=ring_recv.at[way, step, sub],
            device_id=up if way == 0 else down,
            device_id_type=MESH,
        )

    def pair_copy(offset, half):
        origin = lax.rem(z + offset, n_col)
        return pltpu.make_async_remote_copy(
            src_ref=all_basis.at[origin, half],
            dst_ref=all_basis.at[origin, half],
            send_sem=pair_send.at[offset],
            recv_sem=pair_recv.at[offset],
            device_id={"clu": partner},
            device_id_type=MESH,
        )

    def service(index):
        step, sub = lax.div(index, SUB), lax.rem(index, SUB)
        for way, count in ((0, plus_steps), (1, minus_steps)):

            @pl.when(step < count)
            def _():
                origin = (
                    lax.rem(z + n_col - step - 1, n_col)
                    if way == 0
                    else lax.rem(z + step + 1, n_col)
                )
                rows = pl.ds(pl.multiple_of(sub * sub_rows, sub_rows), sub_rows)
                pltpu.make_async_remote_copy(
                    src_ref=all_basis.at[origin, core, rows],
                    dst_ref=all_basis.at[origin, core, rows],
                    send_sem=ring_send.at[way, step, sub],
                    recv_sem=ring_recv.at[way, step, sub],
                    device_id=up if way == 0 else down,
                    device_id_type=MESH,
                ).wait_recv()

                @pl.when(step + 1 < count)
                def _():
                    ring_copy(way, step + 1, sub, None).start()

                @pl.when(sub == SUB - 1)
                def _():
                    pair_copy(n_col - step - 1 if way == 0 else step + 1, core).start()

    def move_copy(k):
        other = lax.rem(me + k, n_clu)
        return pltpu.make_async_remote_copy(
            src_ref=move_out.at[other],
            dst_ref=move_in.at[me],
            send_sem=move_send.at[k],
            recv_sem=move_recv.at[k],
            device_id={"clu": other},
            device_id_type=MESH,
        )

    def from_peer(buffer, sems_out, sems_in, axis, k, count, index):
        other = lax.rem(index + count - k, count)
        return pltpu.make_async_remote_copy(
            src_ref=buffer.at[other],
            dst_ref=buffer.at[other],
            send_sem=sems_out.at[k],
            recv_sem=sems_in.at[k],
            device_id={axis: other},
            device_id_type=MESH,
        )

    pl.semaphore_wait(barrier, n_clu + n_col - 2)

    @pl.loop(1, n_col)
    def _(k):
        node_copy(k).start()

    for sub in range(SUB):
        ring_copy(0, 0, sub, basis_ref).start()
        ring_copy(1, 0, sub, basis_ref).start()

    @pl.loop(1, n_clu)
    def _(k):
        move_copy(k).start()

    own_move = pltpu.make_async_copy(move_out.at[me], move_in.at[me], own_sem.at[2])
    own_move.start()

    services = plus_steps * SUB
    early = services // 4

    @pl.loop(0, early)
    def _(index):
        service(index)

    own_nodes.wait()

    @pl.loop(1, n_col)
    def _(k):
        from_peer(all_nodes, node_send, node_recv, "col", k, n_col, z).wait_recv()

    chunk = 128
    parts = source_count // chunk
    for quarter in range(4):
        for origin in range(quarter * n_col // 4, (quarter + 1) * n_col // 4):
            for part in range(parts):
                piece = all_nodes[origin, :, part * chunk : (part + 1) * chunk].astype(jnp.float32)
                turned = jnp.concatenate([piece] * 4, axis=0).T
                rows = pl.ds(part * chunk, chunk)
                wide_nodes[origin, rows, :node_count] = jnp.broadcast_to(
                    turned[:, 0:1], (chunk, node_count)
                )
                wide_nodes[origin, rows, node_count:] = jnp.broadcast_to(
                    turned[:, 1:2], (chunk, node_count)
                )
        service(early + quarter)

    def form_kernel(b):
        own = far_ref[0, b]
        target_x = pos_ref[pl.ds(2 * b, 1), :]
        target_y = pos_ref[pl.ds(2 * b + 1, 1), :]
        for part in range(parts):
            rows = slice(part * chunk, (part + 1) * chunk)
            delta_x = target_x - wide_nodes[own, rows, :node_count]
            delta_y = target_y - wide_nodes[own, rows, node_count:]
            square_x = delta_x * delta_x
            square_y = delta_y * delta_y
            spread = square_x + square_y + EPS_SQUARED
            log_part = -0.5 * jnp.log(spread)
            inverse = 1.0 / spread
            kernels[b, rows, 0:node_count] = (log_part + square_x * inverse).astype(jnp.bfloat16)
            kernels[b, rows, node_count : 2 * node_count] = (
                delta_x * delta_y * inverse
            ).astype(jnp.bfloat16)
            kernels[b, rows, 2 * node_count : 3 * node_count] = (
                log_part + square_y * inverse
            ).astype(jnp.bfloat16)

    begun = early + 4
    rounds = vesicles // 2
    within = min(rounds, services - begun)

    @pl.loop(0, rounds)
    def _(turn):
        @pl.when(turn < within)
        def _():
            service(begun + turn)

        form_kernel(2 * turn)
        form_kernel(2 * turn + 1)

    @pl.loop(begun + within, services)
    def _(index):
        service(index)

    own_basis.wait()

    @pl.loop(1, n_col)
    def _(k):
        pair_copy(k, 1 - core).wait_recv()

    width = 2 * node_count

    def sketch_row(b):
        basis = all_basis[far_ref[0, b]].reshape(2 * rank_count, source_count)
        product = jnp.dot(basis, kernels[b], preferred_element_type=jnp.float32)
        row = product[:rank_count, :width] + product[rank_count:, node_count:]
        high = row.astype(jnp.bfloat16)
        lanes = pl.ds(pl.multiple_of(b * width, width), width)
        split_ref[:rank_count, lanes] = high
        split_ref[rank_count:, lanes] = (row - high.astype(jnp.float32)).astype(jnp.bfloat16)

    @pl.loop(0, vesicles // ROWS)
    def _(turn):
        for at in range(ROWS):
            sketch_row(turn * ROWS + at)

    keeps[2].start()
    split = split_ref[...]
    total = lax.dot_general(
        split, split, (((1,), (1,)), ((), ())), preferred_element_type=jnp.float32
    )
    gram = (
        total[:rank_count, :rank_count]
        + total[:rank_count, rank_count:]
        + total[rank_count:, :rank_count]
        + total[rank_count:, rank_count:]
    )
    half = rank_count // 2
    folded = jnp.concatenate([gram[:half], gram[half:]], axis=1)
    own_rows = half // n_clu
    for row in range(half):
        part_out[row // own_rows, row % own_rows : row % own_rows + 1, :] = folded[row : row + 1]

    def part_copy(k):
        other = lax.rem(me + k, n_clu)
        return pltpu.make_async_remote_copy(
            src_ref=part_out.at[other],
            dst_ref=part_in.at[me],
            send_sem=part_send.at[k],
            recv_sem=part_recv.at[k],
            device_id={"clu": other},
            device_id_type=MESH,
        )

    @pl.loop(1, n_clu)
    def _(k):
        part_copy(k).start()

    own_move.wait()

    @pl.loop(1, n_clu)
    def _(k):
        from_peer(move_in, move_send, move_recv, "clu", k, n_clu, me).wait_recv()

    goals = move_in[:, 1].reshape(slot_rows, node_count)
    goal_shape = (slot_rows, 2 * vesicles)
    part_index = iota(goal_shape, 0) % 4
    goal_lane = iota(goal_shape, 1).astype(jnp.float32)
    goal_value = goals[:, : 2 * vesicles]
    goal_hot = jnp.where(
        (goal_lane == (part_index * vesicles - 1).astype(jnp.float32) + goal_value)
        & (part_index < 2)
        & (goal_value > 0.0),
        1.0,
        0.0,
    )
    goal_nodes[...] = jnp.dot(
        goal_hot, flat, precision=HIGHEST, preferred_element_type=jnp.float32
    ).reshape(n_clu, 8, node_count)

    def near_pair(src):
        turned = move_in[src, 0].T
        goal_tile = goal_nodes[src]
        results = []
        for slot in range(2):
            first = 4 * slot
            delta_x = goal_tile[first : first + 1] - turned[:, first : first + 1]
            delta_y = goal_tile[first + 1 : first + 2] - turned[:, first + 1 : first + 2]
            push_x = turned[:, first + 2 : first + 3]
            push_y = turned[:, first + 3 : first + 4]
            spread = delta_x * delta_x + delta_y * delta_y + EPS_SQUARED
            log_part = -0.5 * jnp.log(spread)
            along = (delta_x * push_x + delta_y * push_y) * (1.0 / spread)
            results.append(jnp.sum(log_part * push_x + delta_x * along, axis=0, keepdims=True))
            results.append(jnp.sum(log_part * push_y + delta_y * along, axis=0, keepdims=True))
            results.append(jnp.zeros((2, node_count), jnp.float32))
        speeds[src] = jnp.concatenate(results, axis=0)

    @pl.loop(0, n_clu // 4)
    def _(turn):
        near_pair(2 * turn)
        near_pair(2 * turn + 1)

    part_in[me] = part_out[me]

    @pl.loop(1, n_clu)
    def _(k):
        from_peer(part_in, part_send, part_recv, "clu", k, n_clu, me).wait_recv()

    line_out[...] = jnp.sum(part_in[...], axis=0)

    def line_copy(k):
        return pltpu.make_async_remote_copy(
            src_ref=line_out,
            dst_ref=line_in.at[z],
            send_sem=line_send.at[k],
            recv_sem=line_recv.at[k],
            device_id={"col": lax.rem(z + k, n_col)},
            device_id_type=MESH,
        )

    @pl.loop(1, n_col)
    def _(k):
        line_copy(k).start()

    @pl.loop(n_clu // 4, n_clu // 2)
    def _(turn):
        near_pair(2 * turn)
        near_pair(2 * turn + 1)

    near = lax.dot_general(
        goal_hot,
        speeds[...].reshape(slot_rows, node_count),
        (((0,), (0,)), ((), ())),
        precision=HIGHEST,
        preferred_element_type=jnp.float32,
    ) * (1.0 / node_count)
    near_ref[rows_x, :] = near[:vesicles]
    near_ref[rows_y, :] = near[vesicles:]
    keeps[1].start()
    line_in[z] = line_out[...]

    @pl.loop(1, n_col)
    def _(k):
        from_peer(line_in, line_send, line_recv, "col", k, n_col, z).wait_recv()

    sum_row[...] = jnp.sum(line_in[...], axis=0)

    def full_copy(k):
        return pltpu.make_async_remote_copy(
            src_ref=sum_row,
            dst_ref=gram_ref.at[me],
            send_sem=full_send.at[k],
            recv_sem=full_recv.at[k],
            device_id={"clu": lax.rem(me + k, n_clu)},
            device_id_type=MESH,
        )

    @pl.loop(1, n_clu)
    def _(k):
        full_copy(k).start()

    gram_ref[me] = sum_row[...]

    @pl.loop(0, services)
    def _(index):
        step, sub = lax.div(index, SUB), lax.rem(index, SUB)
        ring_copy(0, step, sub, None).wait_send()

        @pl.when(step < minus_steps)
        def _():
            ring_copy(1, step, sub, None).wait_send()

    @pl.loop(1, n_col)
    def _(k):
        node_copy(k).wait_send()
        line_copy(k).wait_send()
        pair_copy(k, core).wait_send()

    @pl.loop(1, n_clu)
    def _(k):
        move_copy(k).wait_send()
        part_copy(k).wait_send()

    @pl.loop(1, n_clu)
    def _(k):
        full_copy(k).wait_send()
        from_peer(gram_ref, full_send, full_recv, "clu", k, n_clu, me).wait_recv()

    keeps[3].start()
    for keep in keeps:
        keep.wait()


def lower_inverse(gram):
    rank_count = gram.shape[0]
    square = (rank_count, rank_count)
    eye = jnp.where(iota(square, 0) == iota(square, 1), 1.0, 0.0)
    joined = jnp.concatenate([gram, eye], axis=1)
    width = 2 * rank_count
    count = rank_count // 8
    tiles = [joined[8 * t : 8 * t + 8] for t in range(count)]
    row_of = iota((8, width), 0)
    for first in range(0, rank_count, 4):
        home, spot = divmod(first, 8)
        tile = tiles[home]
        rows = [tile[spot + i : spot + i + 1] for i in range(4)]
        pivot = [
            [
                jnp.broadcast_to(rows[i][:, first + k : first + k + 1], (1, width))
                for k in range(4)
            ]
            for i in range(4)
        ]
        columns = {
            t: [
                jnp.broadcast_to(tiles[t][:, first + k : first + k + 1], (8, width))
                for k in range(4)
            ]
            for t in range(home, count)
        }
        inverses = []
        for i in range(4):
            inverses.append(1.0 / pivot[i][i])
            for m in range(i + 1, 4):
                ratio = pivot[i][m] * inverses[i]
                rows[m] = rows[m] - ratio * rows[i]
                for k in range(m, 4):
                    pivot[m][k] = pivot[m][k] - ratio * pivot[i][k]
        for t in range(home, count):
            factors = []
            for i in range(4):
                value = columns[t][i]
                for q in range(i):
                    value = value - factors[q] * pivot[q][i]
                factors.append(value * inverses[i])
            updated = tiles[t] - (
                (factors[0] * rows[0] + factors[1] * rows[1])
                + (factors[2] * rows[2] + factors[3] * rows[3])
            )
            if t == home:
                updated = jnp.where(row_of > spot + 3, updated, tile)
                for i in range(1, 4):
                    updated = jnp.where(row_of == spot + i, rows[i], updated)
            tiles[t] = updated
    whole = jnp.concatenate(tiles, axis=0)
    pivots = jnp.sum(whole[:, :rank_count] * eye, axis=1, keepdims=True)
    return whole[:, rank_count:] / jnp.sqrt(pivots)


def finish_kernel(
    scale_factor,
    gram_in,
    split_in,
    force_in,
    near_in,
    basis_out,
    force_out,
    near_out,
    gram_ref,
    split_ref,
    force_ref,
    near_ref,
    spread_ref,
    staged,
    sems,
):
    vesicles, rows, node_count = staged.shape
    rank_count = rows // 2
    loads = [
        pltpu.make_async_copy(source, place, sems.at[2 + at])
        for at, (source, place) in enumerate(
            (
                (gram_in, gram_ref),
                (force_in, force_ref),
                (near_in, near_ref),
                (split_in, split_ref),
            )
        )
    ]
    for load in loads:
        load.start()
    loads[0].wait()
    folded = gram_ref[...]
    gram = jnp.concatenate([folded[:, :rank_count], folded[:, rank_count:]], axis=0)
    lower = lower_inverse(gram) * scale_factor
    for load in loads[1:]:
        load.wait()
    send_force = pltpu.make_async_copy(force_ref, force_out, sems.at[0])
    send_near = pltpu.make_async_copy(near_ref, near_out, sems.at[1])
    send_force.start()
    send_near.start()
    zeros = jnp.zeros_like(lower)
    spread_ref[pl.ds(0, rank_count, stride=2), :] = jnp.concatenate([lower, zeros], axis=1)
    spread_ref[pl.ds(1, rank_count, stride=2), :] = jnp.concatenate([zeros, lower], axis=1)
    spread = spread_ref[...]
    high = spread.astype(jnp.bfloat16)
    low = (spread - high.astype(jnp.float32)).astype(jnp.bfloat16)
    factors = jnp.concatenate([high, low, high, low], axis=1)
    group = 4
    sends = []
    for first in range(0, vesicles, group):
        for b in range(first, first + group):
            lanes = slice(2 * b * node_count, (2 * b + 1) * node_count)
            others = slice((2 * b + 1) * node_count, (2 * b + 2) * node_count)
            upper = [split_ref[:rank_count, lanes], split_ref[:rank_count, others]]
            under = [split_ref[rank_count:, lanes], split_ref[rank_count:, others]]
            staged[b] = jnp.dot(
                factors,
                jnp.concatenate(upper + upper + under + under, axis=0),
                preferred_element_type=jnp.float32,
            )
        rows_now = pl.ds(first, group)
        send = pltpu.make_async_copy(
            staged.at[rows_now], basis_out.at[rows_now], sems.at[6 + first // group]
        )
        send.start()
        sends.append(send)
    for send in sends:
        send.wait()
    send_force.wait()
    send_near.wait()


def per_device(
    positions,
    tension,
    bending,
    moved_order,
    move_destination,
    move_target,
    far_range,
    old_basis,
    source_nodes,
):
    n_clu, n_col = lax.axis_size("clu"), lax.axis_size("col")
    vesicles, node_count = positions.shape[0], positions.shape[2]
    move_count = move_target.shape[0]
    rank_count, source_count = old_basis.shape[0] // 2, old_basis.shape[1]
    half = rank_count // 2
    own_rows = half // n_clu
    plus_steps = n_col // 2
    f32, bf16, i32 = jnp.float32, jnp.bfloat16, jnp.int32
    vmem, dma = pltpu.VMEM, pltpu.SemaphoreType.DMA
    in_hbm = pl.BlockSpec(memory_space=pltpu.HBM)
    sizes = (n_clu, n_col, vesicles, node_count, move_count, rank_count, source_count)
    flat_shape = jax.ShapeDtypeStruct((2 * vesicles, node_count), f32)
    force, near, split, gram = pl.pallas_call(
        functools.partial(main_kernel, sizes),
        out_shape=(
            flat_shape,
            flat_shape,
            jax.ShapeDtypeStruct((2 * rank_count, vesicles * 2 * node_count), bf16),
            jax.ShapeDtypeStruct((n_clu, own_rows, 2 * rank_count), f32),
        ),
        in_specs=[in_hbm] * 10,
        out_specs=[in_hbm] * 4,
        scratch_shapes=[
            vmem((2 * vesicles, node_count), f32),
            vmem((2 * vesicles, node_count), f32),
            vmem((2 * rank_count, vesicles * 2 * node_count), bf16),
            vmem((n_clu, own_rows, 2 * rank_count), f32),
            pltpu.SMEM((1, vesicles), i32),
            vmem((node_count, 2 * node_count), f32),
            vmem((2 * vesicles, node_count), f32),
            vmem((vesicles, node_count), f32),
            vmem((1, vesicles), f32),
            vmem((1, vesicles), i32),
            vmem((1, move_count), i32),
            vmem((1, move_count), i32),
            vmem((n_clu, 2, 8, node_count), f32),
            vmem((n_clu, 2, 8, node_count), f32),
            vmem((n_clu, 8, node_count), f32),
            vmem((n_clu, 8, node_count), f32),
            vmem((n_col, 2, rank_count, source_count), bf16),
            vmem((n_col, 2, source_count), bf16),
            vmem((n_col, source_count, 2 * node_count), f32),
            vmem((vesicles, source_count, 3 * node_count), bf16),
            vmem((n_clu, own_rows, 2 * rank_count), f32),
            vmem((n_clu, own_rows, 2 * rank_count), f32),
            vmem((own_rows, 2 * rank_count), f32),
            vmem((n_col, own_rows, 2 * rank_count), f32),
            vmem((own_rows, 2 * rank_count), f32),
            dma((n_clu,)),
            dma((n_clu,)),
            dma((n_col,)),
            dma((n_col,)),
            dma((2, plus_steps, SUB)),
            dma((2, plus_steps, SUB)),
            dma((n_col,)),
            dma((n_col,)),
            dma((15,)),
            dma((n_clu,)),
            dma((n_clu,)),
            dma((n_col,)),
            dma((n_col,)),
            dma((n_clu,)),
            dma((n_clu,)),
        ],
        compiler_params=pltpu.CompilerParams(
            collective_id=0, has_side_effects=True, vmem_limit_bytes=VMEM_ALL
        ),
        name="main_step",
    )(
        far_range.reshape(1, vesicles),
        jnp.asarray(spectral_tables(node_count)),
        positions.reshape(2 * vesicles, node_count),
        tension,
        bending.reshape(1, vesicles),
        moved_order,
        move_destination.reshape(1, move_count),
        move_target.reshape(1, move_count),
        old_basis.reshape(2, rank_count, source_count),
        source_nodes,
    )
    scale_factor = math.sqrt(2.0 * node_count * vesicles * n_clu * n_col)
    new_basis, force, near = pl.pallas_call(
        functools.partial(finish_kernel, scale_factor),
        out_shape=(
            jax.ShapeDtypeStruct((vesicles, 2 * rank_count, node_count), f32),
            flat_shape,
            flat_shape,
        ),
        in_specs=[in_hbm] * 4,
        out_specs=[in_hbm] * 3,
        scratch_shapes=[
            vmem((half, 2 * rank_count), f32),
            vmem((2 * rank_count, vesicles * 2 * node_count), bf16),
            vmem((2 * vesicles, node_count), f32),
            vmem((2 * vesicles, node_count), f32),
            vmem((2 * rank_count, 2 * rank_count), f32),
            vmem((vesicles, 2 * rank_count, node_count), f32),
            dma((6 + vesicles // 4,)),
        ],
        compiler_params=pltpu.CompilerParams(vmem_limit_bytes=VMEM_ALL),
        name="finish_step",
    )(gram.reshape(half, 2 * rank_count), split, force, near)
    return (
        force.reshape(vesicles, 2, node_count),
        near.reshape(vesicles, 2, node_count),
        new_basis.reshape(vesicles, rank_count, 2, node_count),
    )


def solution(mesh):
    placed = (
        P(("clu", "col"), None, None),
        P(("clu", "col"), None),
        P(("clu", "col")),
        P(("clu", "col"), None),
        P(("clu", "col"), None),
        P(("clu", "col")),
        P(("clu", "col"), None),
        P(None, "col"),
        P(None, "col"),
    )
    return jax.shard_map(
        per_device,
        mesh=mesh,
        in_specs=placed,
        out_specs=(
            P(("clu", "col"), None, None),
            P(("clu", "col"), None, None),
            P(("clu", "col"), None, None, None),
        ),
        check_vma=False,
    )
```

```python
import functools
import math

import jax
import jax.numpy as jnp
import numpy as np
from jax import lax
from jax.experimental import pallas as pl
from jax.experimental.pallas import tpu as pltpu
from jax.sharding import PartitionSpec as P

EPS_SQUARED = 0.01
HIGHEST = lax.Precision.HIGHEST
MESH = pl.DeviceIdType.MESH
CHIPS_X = 4
LAG = 6
MOVE_TURN = 12
DELAY = 4
ROWS = 8
VMEM_ALL = 67043328


def spectral_tables(node_count):
    half_count = node_count // 2
    node_index = np.arange(node_count)[:, None]
    wave_index = np.arange(half_count + 1)[None, :]
    phase_angle = (node_index * wave_index % node_count) * (2.0 * math.pi / node_count)
    cosine_table = np.cos(phase_angle)
    sine_table = np.sin(phase_angle)
    wavenumber = np.arange(half_count + 1).astype(np.float64)
    inside = (wavenumber > 0) & (wavenumber < half_count)
    first_weight = np.where(inside, 2.0 * wavenumber / half_count, 0.0)
    fourth_weight = np.where(
        inside, 2.0 * (wavenumber / half_count) ** 4, np.where(wavenumber == half_count, 1.0, 0.0)
    )
    derivative = (
        (cosine_table * first_weight) @ sine_table.T - (sine_table * first_weight) @ cosine_table.T
    ) / node_count
    bending_table = (
        (cosine_table * fourth_weight) @ cosine_table.T
        + (sine_table * fourth_weight) @ sine_table.T
    ) / node_count
    return np.concatenate([derivative.T, bending_table.T], axis=1).astype(np.float32)


def iota(shape, dim):
    return lax.broadcasted_iota(jnp.int32, shape, dim)


def main_kernel(
    sizes,
    far_hbm,
    table_hbm,
    pos_hbm,
    tension_hbm,
    bending_hbm,
    order_hbm,
    dest_hbm,
    goal_hbm,
    basis_ref,
    nodes_hbm,
    force_out,
    near_out,
    split_out,
    gram_out,
    force_ref,
    near_ref,
    split_ref,
    gram_ref,
    far_ref,
    table_ref,
    pos_ref,
    tension_ref,
    bending_ref,
    order_ref,
    dest_ref,
    goal_ref,
    move_out,
    move_in,
    goal_nodes,
    speeds,
    all_basis,
    all_nodes,
    wide_nodes,
    kernels,
    part_out,
    part_in,
    line_out,
    line_in,
    sum_row,
    move_send,
    move_recv,
    node_send,
    node_recv,
    ring_send,
    ring_recv,
    first_send,
    first_recv,
    second_send,
    second_recv,
    pair_send,
    pair_recv,
    own_sem,
    part_send,
    part_recv,
    line_send,
    line_recv,
    full_send,
    full_recv,
):
    n_clu, n_col, vesicles, node_count, move_count, rank_count, source_count = sizes
    me = lax.axis_index("clu")
    z = lax.axis_index("col")
    core = lax.rem(me, 2)
    partner = me + 1 - 2 * core
    chips = min(CHIPS_X, n_clu // 2)
    members = 2 * chips
    plane = lax.div(me, members)
    across = lax.div(lax.rem(me, members), 2)
    major = across + core * (plane - across)
    minor = plane + core * (across - plane)
    lane_share = source_count // chips

    barrier = pltpu.get_barrier_semaphore()

    @pl.loop(1, n_col)
    def _(k):
        pl.semaphore_signal(
            barrier, inc=1, device_id={"col": lax.rem(z + k, n_col)}, device_id_type=MESH
        )

    @pl.loop(1, n_clu)
    def _(k):
        pl.semaphore_signal(
            barrier, inc=1, device_id={"clu": lax.rem(me + k, n_clu)}, device_id_type=MESH
        )

    loads = [
        pltpu.make_async_copy(source, place, own_sem.at[3 + at])
        for at, (source, place) in enumerate(
            (
                (pos_hbm, pos_ref),
                (table_hbm, table_ref),
                (tension_hbm, tension_ref),
                (bending_hbm, bending_ref),
                (order_hbm, order_ref),
                (dest_hbm, dest_ref),
                (goal_hbm, goal_ref),
                (far_hbm, far_ref),
            )
        )
    ]
    for load in loads:
        load.start()
    keeps = [
        pltpu.make_async_copy(source, place, own_sem.at[11 + at])
        for at, (source, place) in enumerate(
            (
                (force_ref, force_out),
                (near_ref, near_out),
                (split_ref, split_out),
                (gram_ref, gram_out),
            )
        )
    ]
    own_basis = pltpu.make_async_copy(basis_ref, all_basis.at[z], own_sem.at[0])
    own_basis.start()
    load_nodes = pltpu.make_async_copy(nodes_hbm, all_nodes.at[z], own_sem.at[1])
    load_nodes.start()
    load_nodes.wait()
    for load in loads:
        load.wait()

    rows_x = pl.ds(0, vesicles, stride=2)
    rows_y = pl.ds(1, vesicles, stride=2)
    flat = jnp.concatenate([pos_ref[rows_x, :], pos_ref[rows_y, :]], axis=0)
    table = table_ref[...]
    both = jnp.dot(flat, table, precision=HIGHEST, preferred_element_type=jnp.float32)
    slope = both[:, :node_count]
    fourth = both[:, node_count:]
    tension = tension_ref[...]
    pulled = slope * jnp.concatenate([tension, tension], axis=0)
    stretch = jnp.dot(
        pulled, table[:, :node_count], precision=HIGHEST, preferred_element_type=jnp.float32
    )
    square = (vesicles, vesicles)
    bending = jnp.sum(
        jnp.where(iota(square, 0) == iota(square, 1), bending_ref[...], 0.0), axis=1, keepdims=True
    )
    force = stretch - jnp.concatenate([bending, bending], axis=0) * fourth
    force_ref[rows_x, :] = force[:vesicles]
    force_ref[rows_y, :] = force[vesicles:]
    keeps[0].start()
    carried = jnp.concatenate([flat, force], axis=0)

    pairs = (move_count, move_count)
    dest_row = dest_ref[...].astype(jnp.float32)
    dest_col = jnp.sum(
        jnp.where(iota(pairs, 0) == iota(pairs, 1), dest_row, 0.0), axis=1, keepdims=True
    )
    earlier = jnp.sum(
        jnp.where((dest_col == dest_row) & (iota(pairs, 0) < iota(pairs, 1)), 1.0, 0.0),
        axis=0,
        keepdims=True,
    )
    slot_rows = n_clu * 8
    wide = (slot_rows, move_count)
    match = (dest_row == (iota(wide, 0) // 8).astype(jnp.float32)) & (
        earlier == (iota(wide, 0) // 4 % 2).astype(jnp.float32)
    )
    order_row = order_ref[:, :move_count].astype(jnp.float32)
    goal_row = goal_ref[...].astype(jnp.float32) + 1.0
    found = jnp.sum(jnp.where(match, 1.0, 0.0), axis=1, keepdims=True)
    chosen = jnp.sum(jnp.where(match, order_row, 0.0), axis=1, keepdims=True)
    goal = jnp.sum(jnp.where(match, goal_row, 0.0), axis=1, keepdims=True)
    table_shape = (slot_rows, 4 * vesicles)
    part_first = (iota(table_shape, 0) % 4 * vesicles).astype(jnp.float32)
    lane = iota(table_shape, 1).astype(jnp.float32)
    pack = jnp.where((lane == part_first + chosen) & (found > 0.0), 1.0, 0.0)
    packed = jnp.dot(pack, carried, precision=HIGHEST, preferred_element_type=jnp.float32)
    move_out[:, 0] = packed.reshape(n_clu, 8, node_count)
    move_out[:, 1] = jnp.broadcast_to(goal, (slot_rows, node_count)).reshape(n_clu, 8, node_count)

    def node_copy(k):
        return pltpu.make_async_remote_copy(
            src_ref=nodes_hbm,
            dst_ref=all_nodes.at[z],
            send_sem=node_send.at[k],
            recv_sem=node_recv.at[k],
            device_id={"col": lax.rem(z + k, n_col)},
            device_id_type=MESH,
        )

    def line_offset(turn):
        odd = lax.rem(turn, 2)
        return (1 - odd) * (lax.div(turn, 2) + 1) + odd * (n_col - lax.div(turn + 1, 2))

    def peer(down, right):
        first = lax.rem(minor + down, chips)
        second = lax.rem(major + right, chips)
        return {
            "clu": (first + core * (second - first)) * members
            + 2 * (second + core * (first - second))
            + core
        }

    def tile(ref, row, column):
        lanes = pl.ds(pl.multiple_of(column * lane_share, lane_share), lane_share)
        return ref.at[core, row, :, lanes]

    def origin_of(k):
        return lax.rem(z + n_col - k, n_col)

    def ring_copy(k):
        return pltpu.make_async_remote_copy(
            src_ref=tile(basis_ref, major, minor),
            dst_ref=tile(all_basis.at[z], major, minor),
            send_sem=ring_send.at[k],
            recv_sem=ring_recv.at[k],
            device_id={"col": lax.rem(z + k, n_col)},
            device_id_type=MESH,
        )

    def from_ring(k):
        block = tile(all_basis.at[origin_of(k)], major, minor)
        return pltpu.make_async_remote_copy(
            src_ref=block,
            dst_ref=block,
            send_sem=ring_send.at[k],
            recv_sem=ring_recv.at[k],
            device_id={"col": origin_of(k)},
            device_id_type=MESH,
        )

    def first_copy(k, d, back):
        column = lax.rem(minor + back * (chips - d), chips)
        block = tile(all_basis.at[origin_of(k)], major, column)
        return pltpu.make_async_remote_copy(
            src_ref=block,
            dst_ref=block,
            send_sem=first_send.at[k, d],
            recv_sem=first_recv.at[k, d],
            device_id=peer(chips - d if back else d, 0),
            device_id_type=MESH,
        )

    def second_copy(k, d, back):
        row = lax.rem(major + back * (chips - d), chips)
        block = all_basis.at[origin_of(k), core, row]
        return pltpu.make_async_remote_copy(
            src_ref=block,
            dst_ref=block,
            send_sem=second_send.at[k, d],
            recv_sem=second_recv.at[k, d],
            device_id=peer(0, chips - d if back else d),
            device_id_type=MESH,
        )

    def pair_copy(k, half):
        block = all_basis.at[origin_of(k), half]
        return pltpu.make_async_remote_copy(
            src_ref=block,
            dst_ref=block,
            send_sem=pair_send.at[k],
            recv_sem=pair_recv.at[k],
            device_id={"clu": partner},
            device_id_type=MESH,
        )

    def service(turn):
        @pl.when(turn < n_col - 1)
        def _():
            k = line_offset(turn)
            from_ring(k).wait_recv()
            for d in range(1, chips):
                first_copy(k, d, 0).start()

        @pl.when((turn >= LAG) & (turn < n_col - 1 + LAG))
        def _():
            k = line_offset(turn - LAG)
            for d in range(1, chips):
                first_copy(k, d, 1).wait_recv()
            for d in range(1, chips):
                second_copy(k, d, 0).start()

        @pl.when(turn >= 2 * LAG)
        def _():
            k = line_offset(turn - 2 * LAG)
            for d in range(1, chips):
                second_copy(k, d, 1).wait_recv()
            pair_copy(k, core).start()

    def move_copy(k):
        other = lax.rem(me + k, n_clu)
        return pltpu.make_async_remote_copy(
            src_ref=move_out.at[other],
            dst_ref=move_in.at[me],
            send_sem=move_send.at[k],
            recv_sem=move_recv.at[k],
            device_id={"clu": other},
            device_id_type=MESH,
        )

    def from_peer(buffer, sems_out, sems_in, axis, k, count, index):
        other = lax.rem(index + count - k, count)
        return pltpu.make_async_remote_copy(
            src_ref=buffer.at[other],
            dst_ref=buffer.at[other],
            send_sem=sems_out.at[k],
            recv_sem=sems_in.at[k],
            device_id={axis: other},
            device_id_type=MESH,
        )

    pl.semaphore_wait(barrier, n_clu + n_col - 2)

    @pl.loop(1, n_col)
    def _(k):
        node_copy(k).start()

    @pl.loop(0, n_col - 1)
    def _(turn):
        ring_copy(line_offset(turn)).start()

    services = n_col - 1 + 2 * LAG
    early = n_col - 1 - DELAY
    chunk = 128
    parts = source_count // chunk

    def widen(origin):
        nodes = all_nodes[origin].astype(jnp.float32)
        for part in range(parts):
            piece = nodes[:, part * chunk : (part + 1) * chunk]
            turned = jnp.concatenate([piece] * 4, axis=0).T
            rows = slice(part * chunk, (part + 1) * chunk)
            wide_nodes[origin, rows, :node_count] = jnp.broadcast_to(
                turned[:, 0:1], (chunk, node_count)
            )
            wide_nodes[origin, rows, node_count:] = jnp.broadcast_to(
                turned[:, 1:2], (chunk, node_count)
            )

    widen(z)

    @pl.loop(0, n_col - 1)
    def _(turn):
        k = line_offset(turn)
        from_peer(all_nodes, node_send, node_recv, "col", k, n_col, z).wait_recv()
        widen(origin_of(k))

        @pl.when(turn >= DELAY)
        def _():
            service(turn - DELAY)

    def form_kernel(b):
        own = far_ref[0, b]
        target_x = pos_ref[pl.ds(2 * b, 1), :]
        target_y = pos_ref[pl.ds(2 * b + 1, 1), :]
        for part in range(parts):
            rows = slice(part * chunk, (part + 1) * chunk)
            delta_x = target_x - wide_nodes[own, rows, :node_count]
            delta_y = target_y - wide_nodes[own, rows, node_count:]
            square_x = delta_x * delta_x
            square_y = delta_y * delta_y
            spread = square_x + square_y + EPS_SQUARED
            log_part = -0.5 * jnp.log(spread)
            inverse = 1.0 / spread
            kernels[b, rows, 0:node_count] = (log_part + square_x * inverse).astype(jnp.bfloat16)
            kernels[b, rows, node_count : 2 * node_count] = (
                delta_x * delta_y * inverse
            ).astype(jnp.bfloat16)
            kernels[b, rows, 2 * node_count : 3 * node_count] = (
                log_part + square_y * inverse
            ).astype(jnp.bfloat16)

    own_move = pltpu.make_async_copy(move_out.at[me], move_in.at[me], own_sem.at[2])
    own_move.start()
    begun = early
    rounds = vesicles // 2
    within = min(rounds, services - begun)

    @pl.loop(0, rounds)
    def _(turn):
        form_kernel(2 * turn)
        form_kernel(2 * turn + 1)

        @pl.when(turn < within)
        def _():
            service(begun + turn)

        @pl.when(turn == min(MOVE_TURN, rounds - 1))
        def _():
            @pl.loop(1, n_clu)
            def _(k):
                move_copy(k).start()

    @pl.loop(begun + within, services)
    def _(index):
        service(index)

    own_basis.wait()

    @pl.loop(1, n_col)
    def _(k):
        pair_copy(k, 1 - core).wait_recv()

    width = 2 * node_count

    def sketch_row(b):
        basis = all_basis[far_ref[0, b]].reshape(2 * rank_count, source_count)
        product = jnp.dot(basis, kernels[b], preferred_element_type=jnp.float32)
        row = product[:rank_count, :width] + product[rank_count:, node_count:]
        high = row.astype(jnp.bfloat16)
        lanes = pl.ds(pl.multiple_of(b * width, width), width)
        split_ref[:rank_count, lanes] = high
        split_ref[rank_count:, lanes] = (row - high.astype(jnp.float32)).astype(jnp.bfloat16)

    @pl.loop(0, vesicles // ROWS)
    def _(turn):
        for at in range(ROWS):
            sketch_row(turn * ROWS + at)

    keeps[2].start()
    split = split_ref[...]
    total = lax.dot_general(
        split, split, (((1,), (1,)), ((), ())), preferred_element_type=jnp.float32
    )
    gram = (
        total[:rank_count, :rank_count]
        + total[:rank_count, rank_count:]
        + total[rank_count:, :rank_count]
        + total[rank_count:, rank_count:]
    )
    half = rank_count // 2
    folded = jnp.concatenate([gram[:half], gram[half:]], axis=1)
    own_rows = half // n_clu
    for row in range(half):
        part_out[row // own_rows, row % own_rows : row % own_rows + 1, :] = folded[row : row + 1]

    def part_copy(k):
        other = lax.rem(me + k, n_clu)
        return pltpu.make_async_remote_copy(
            src_ref=part_out.at[other],
            dst_ref=part_in.at[me],
            send_sem=part_send.at[k],
            recv_sem=part_recv.at[k],
            device_id={"clu": other},
            device_id_type=MESH,
        )

    @pl.loop(1, n_clu)
    def _(k):
        part_copy(k).start()

    own_move.wait()

    @pl.loop(1, n_clu)
    def _(k):
        from_peer(move_in, move_send, move_recv, "clu", k, n_clu, me).wait_recv()

    goals = move_in[:, 1].reshape(slot_rows, node_count)
    goal_shape = (slot_rows, 2 * vesicles)
    part_index = iota(goal_shape, 0) % 4
    goal_lane = iota(goal_shape, 1).astype(jnp.float32)
    goal_value = goals[:, : 2 * vesicles]
    goal_hot = jnp.where(
        (goal_lane == (part_index * vesicles - 1).astype(jnp.float32) + goal_value)
        & (part_index < 2)
        & (goal_value > 0.0),
        1.0,
        0.0,
    )
    goal_nodes[...] = jnp.dot(
        goal_hot, flat, precision=HIGHEST, preferred_element_type=jnp.float32
    ).reshape(n_clu, 8, node_count)

    def near_pair(src):
        turned = move_in[src, 0].T
        goal_tile = goal_nodes[src]
        results = []
        for slot in range(2):
            first = 4 * slot
            delta_x = goal_tile[first : first + 1] - turned[:, first : first + 1]
            delta_y = goal_tile[first + 1 : first + 2] - turned[:, first + 1 : first + 2]
            push_x = turned[:, first + 2 : first + 3]
            push_y = turned[:, first + 3 : first + 4]
            spread = delta_x * delta_x + delta_y * delta_y + EPS_SQUARED
            log_part = -0.5 * jnp.log(spread)
            along = (delta_x * push_x + delta_y * push_y) * (1.0 / spread)
            results.append(jnp.sum(log_part * push_x + delta_x * along, axis=0, keepdims=True))
            results.append(jnp.sum(log_part * push_y + delta_y * along, axis=0, keepdims=True))
            results.append(jnp.zeros((2, node_count), jnp.float32))
        speeds[src] = jnp.concatenate(results, axis=0)

    @pl.loop(0, n_clu // 4)
    def _(turn):
        near_pair(2 * turn)
        near_pair(2 * turn + 1)

    part_in[me] = part_out[me]

    @pl.loop(1, n_clu)
    def _(k):
        from_peer(part_in, part_send, part_recv, "clu", k, n_clu, me).wait_recv()

    line_out[...] = jnp.sum(part_in[...], axis=0)

    def line_copy(k):
        return pltpu.make_async_remote_copy(
            src_ref=line_out,
            dst_ref=line_in.at[z],
            send_sem=line_send.at[k],
            recv_sem=line_recv.at[k],
            device_id={"col": lax.rem(z + k, n_col)},
            device_id_type=MESH,
        )

    @pl.loop(1, n_col)
    def _(k):
        line_copy(k).start()

    @pl.loop(n_clu // 4, n_clu // 2)
    def _(turn):
        near_pair(2 * turn)
        near_pair(2 * turn + 1)

    near = lax.dot_general(
        goal_hot,
        speeds[...].reshape(slot_rows, node_count),
        (((0,), (0,)), ((), ())),
        precision=HIGHEST,
        preferred_element_type=jnp.float32,
    ) * (1.0 / node_count)
    near_ref[rows_x, :] = near[:vesicles]
    near_ref[rows_y, :] = near[vesicles:]
    keeps[1].start()
    line_in[z] = line_out[...]

    @pl.loop(1, n_col)
    def _(k):
        from_peer(line_in, line_send, line_recv, "col", k, n_col, z).wait_recv()

    sum_row[...] = jnp.sum(line_in[...], axis=0)

    def full_copy(k):
        return pltpu.make_async_remote_copy(
            src_ref=sum_row,
            dst_ref=gram_ref.at[me],
            send_sem=full_send.at[k],
            recv_sem=full_recv.at[k],
            device_id={"clu": lax.rem(me + k, n_clu)},
            device_id_type=MESH,
        )

    @pl.loop(1, n_clu)
    def _(k):
        full_copy(k).start()

    gram_ref[me] = sum_row[...]

    @pl.loop(1, n_col)
    def _(k):
        node_copy(k).wait_send()
        line_copy(k).wait_send()
        pair_copy(k, core).wait_send()
        ring_copy(k).wait_send()
        for d in range(1, chips):
            first_copy(k, d, 0).wait_send()
            second_copy(k, d, 0).wait_send()

    @pl.loop(1, n_clu)
    def _(k):
        move_copy(k).wait_send()
        part_copy(k).wait_send()

    @pl.loop(1, n_clu)
    def _(k):
        full_copy(k).wait_send()
        from_peer(gram_ref, full_send, full_recv, "clu", k, n_clu, me).wait_recv()

    keeps[3].start()
    for keep in keeps:
        keep.wait()


def lower_inverse(gram):
    rank_count = gram.shape[0]
    square = (rank_count, rank_count)
    eye = jnp.where(iota(square, 0) == iota(square, 1), 1.0, 0.0)
    joined = jnp.concatenate([gram, eye], axis=1)
    width = 2 * rank_count
    count = rank_count // 8
    tiles = [joined[8 * t : 8 * t + 8] for t in range(count)]
    row_of = iota((8, width), 0)
    for first in range(0, rank_count, 4):
        home, spot = divmod(first, 8)
        tile = tiles[home]
        rows = [tile[spot + i : spot + i + 1] for i in range(4)]
        pivot = [
            [
                jnp.broadcast_to(rows[i][:, first + k : first + k + 1], (1, width))
                for k in range(4)
            ]
            for i in range(4)
        ]
        columns = {
            t: [
                jnp.broadcast_to(tiles[t][:, first + k : first + k + 1], (8, width))
                for k in range(4)
            ]
            for t in range(home, count)
        }
        inverses = []
        for i in range(4):
            inverses.append(1.0 / pivot[i][i])
            for m in range(i + 1, 4):
                ratio = pivot[i][m] * inverses[i]
                rows[m] = rows[m] - ratio * rows[i]
                for k in range(m, 4):
                    pivot[m][k] = pivot[m][k] - ratio * pivot[i][k]
        for t in range(home, count):
            factors = []
            for i in range(4):
                value = columns[t][i]
                for q in range(i):
                    value = value - factors[q] * pivot[q][i]
                factors.append(value * inverses[i])
            updated = tiles[t] - (
                (factors[0] * rows[0] + factors[1] * rows[1])
                + (factors[2] * rows[2] + factors[3] * rows[3])
            )
            if t == home:
                updated = jnp.where(row_of > spot + 3, updated, tile)
                for i in range(1, 4):
                    updated = jnp.where(row_of == spot + i, rows[i], updated)
            tiles[t] = updated
    whole = jnp.concatenate(tiles, axis=0)
    pivots = jnp.sum(whole[:, :rank_count] * eye, axis=1, keepdims=True)
    return whole[:, rank_count:] / jnp.sqrt(pivots)


def finish_kernel(
    scale_factor,
    gram_in,
    split_in,
    force_in,
    near_in,
    basis_out,
    force_out,
    near_out,
    gram_ref,
    split_ref,
    force_ref,
    near_ref,
    spread_ref,
    staged,
    sems,
):
    vesicles, rows, node_count = staged.shape
    rank_count = rows // 2
    loads = [
        pltpu.make_async_copy(source, place, sems.at[2 + at])
        for at, (source, place) in enumerate(
            (
                (gram_in, gram_ref),
                (force_in, force_ref),
                (near_in, near_ref),
                (split_in, split_ref),
            )
        )
    ]
    for load in loads:
        load.start()
    loads[0].wait()
    folded = gram_ref[...]
    gram = jnp.concatenate([folded[:, :rank_count], folded[:, rank_count:]], axis=0)
    lower = lower_inverse(gram) * scale_factor
    for load in loads[1:]:
        load.wait()
    send_force = pltpu.make_async_copy(force_ref, force_out, sems.at[0])
    send_near = pltpu.make_async_copy(near_ref, near_out, sems.at[1])
    send_force.start()
    send_near.start()
    zeros = jnp.zeros_like(lower)
    spread_ref[pl.ds(0, rank_count, stride=2), :] = jnp.concatenate([lower, zeros], axis=1)
    spread_ref[pl.ds(1, rank_count, stride=2), :] = jnp.concatenate([zeros, lower], axis=1)
    spread = spread_ref[...]
    high = spread.astype(jnp.bfloat16)
    low = (spread - high.astype(jnp.float32)).astype(jnp.bfloat16)
    factors = jnp.concatenate([high, low, high, low], axis=1)
    group = 4
    sends = []
    for first in range(0, vesicles, group):
        for b in range(first, first + group):
            lanes = slice(2 * b * node_count, (2 * b + 1) * node_count)
            others = slice((2 * b + 1) * node_count, (2 * b + 2) * node_count)
            upper = [split_ref[:rank_count, lanes], split_ref[:rank_count, others]]
            under = [split_ref[rank_count:, lanes], split_ref[rank_count:, others]]
            staged[b] = jnp.dot(
                factors,
                jnp.concatenate(upper + upper + under + under, axis=0),
                preferred_element_type=jnp.float32,
            )
        rows_now = pl.ds(first, group)
        send = pltpu.make_async_copy(
            staged.at[rows_now], basis_out.at[rows_now], sems.at[6 + first // group]
        )
        send.start()
        sends.append(send)
    for send in sends:
        send.wait()
    send_force.wait()
    send_near.wait()


def per_device(
    positions,
    tension,
    bending,
    moved_order,
    move_destination,
    move_target,
    far_range,
    old_basis,
    source_nodes,
):
    n_clu, n_col = lax.axis_size("clu"), lax.axis_size("col")
    vesicles, node_count = positions.shape[0], positions.shape[2]
    move_count = move_target.shape[0]
    rank_count, source_count = old_basis.shape[0] // 2, old_basis.shape[1]
    half = rank_count // 2
    own_rows = half // n_clu
    chips = min(CHIPS_X, n_clu // 2)
    row_share = rank_count // chips
    f32, bf16, i32 = jnp.float32, jnp.bfloat16, jnp.int32
    vmem, dma = pltpu.VMEM, pltpu.SemaphoreType.DMA
    in_hbm = pl.BlockSpec(memory_space=pltpu.HBM)
    sizes = (n_clu, n_col, vesicles, node_count, move_count, rank_count, source_count)
    flat_shape = jax.ShapeDtypeStruct((2 * vesicles, node_count), f32)
    force, near, split, gram = pl.pallas_call(
        functools.partial(main_kernel, sizes),
        out_shape=(
            flat_shape,
            flat_shape,
            jax.ShapeDtypeStruct((2 * rank_count, vesicles * 2 * node_count), bf16),
            jax.ShapeDtypeStruct((n_clu, own_rows, 2 * rank_count), f32),
        ),
        in_specs=[in_hbm] * 10,
        out_specs=[in_hbm] * 4,
        scratch_shapes=[
            vmem((2 * vesicles, node_count), f32),
            vmem((2 * vesicles, node_count), f32),
            vmem((2 * rank_count, vesicles * 2 * node_count), bf16),
            vmem((n_clu, own_rows, 2 * rank_count), f32),
            pltpu.SMEM((1, vesicles), i32),
            vmem((node_count, 2 * node_count), f32),
            vmem((2 * vesicles, node_count), f32),
            vmem((vesicles, node_count), f32),
            vmem((1, vesicles), f32),
            vmem((1, vesicles), i32),
            vmem((1, move_count), i32),
            vmem((1, move_count), i32),
            vmem((n_clu, 2, 8, node_count), f32),
            vmem((n_clu, 2, 8, node_count), f32),
            vmem((n_clu, 8, node_count), f32),
            vmem((n_clu, 8, node_count), f32),
            vmem((n_col, 2, chips, row_share, source_count), bf16),
            vmem((n_col, 2, source_count), bf16),
            vmem((n_col, source_count, 2 * node_count), f32),
            vmem((vesicles, source_count, 3 * node_count), bf16),
            vmem((n_clu, own_rows, 2 * rank_count), f32),
            vmem((n_clu, own_rows, 2 * rank_count), f32),
            vmem((own_rows, 2 * rank_count), f32),
            vmem((n_col, own_rows, 2 * rank_count), f32),
            vmem((own_rows, 2 * rank_count), f32),
            dma((n_clu,)),
            dma((n_clu,)),
            dma((n_col,)),
            dma((n_col,)),
            dma((n_col,)),
            dma((n_col,)),
            dma((n_col, chips)),
            dma((n_col, chips)),
            dma((n_col, chips)),
            dma((n_col, chips)),
            dma((n_col,)),
            dma((n_col,)),
            dma((15,)),
            dma((n_clu,)),
            dma((n_clu,)),
            dma((n_col,)),
            dma((n_col,)),
            dma((n_clu,)),
            dma((n_clu,)),
        ],
        compiler_params=pltpu.CompilerParams(
            collective_id=0, has_side_effects=True, vmem_limit_bytes=VMEM_ALL
        ),
        name="main_step",
    )(
        far_range.reshape(1, vesicles),
        jnp.asarray(spectral_tables(node_count)),
        positions.reshape(2 * vesicles, node_count),
        tension,
        bending.reshape(1, vesicles),
        moved_order,
        move_destination.reshape(1, move_count),
        move_target.reshape(1, move_count),
        old_basis.reshape(2, chips, row_share, source_count),
        source_nodes,
    )
    scale_factor = math.sqrt(2.0 * node_count * vesicles * n_clu * n_col)
    new_basis, force, near = pl.pallas_call(
        functools.partial(finish_kernel, scale_factor),
        out_shape=(
            jax.ShapeDtypeStruct((vesicles, 2 * rank_count, node_count), f32),
            flat_shape,
            flat_shape,
        ),
        in_specs=[in_hbm] * 4,
        out_specs=[in_hbm] * 3,
        scratch_shapes=[
            vmem((half, 2 * rank_count), f32),
            vmem((2 * rank_count, vesicles * 2 * node_count), bf16),
            vmem((2 * vesicles, node_count), f32),
            vmem((2 * vesicles, node_count), f32),
            vmem((2 * rank_count, 2 * rank_count), f32),
            vmem((vesicles, 2 * rank_count, node_count), f32),
            dma((6 + vesicles // 4,)),
        ],
        compiler_params=pltpu.CompilerParams(vmem_limit_bytes=VMEM_ALL),
        name="finish_step",
    )(gram.reshape(half, 2 * rank_count), split, force, near)
    return (
        force.reshape(vesicles, 2, node_count),
        near.reshape(vesicles, 2, node_count),
        new_basis.reshape(vesicles, rank_count, 2, node_count),
    )


def solution(mesh):
    placed = (
        P(("clu", "col"), None, None),
        P(("clu", "col"), None),
        P(("clu", "col")),
        P(("clu", "col"), None),
        P(("clu", "col"), None),
        P(("clu", "col")),
        P(("clu", "col"), None),
        P(None, "col"),
        P(None, "col"),
    )
    return jax.shard_map(
        per_device,
        mesh=mesh,
        in_specs=placed,
        out_specs=(
            P(("clu", "col"), None, None),
            P(("clu", "col"), None, None),
            P(("clu", "col"), None, None, None),
        ),
        check_vma=False,
    )
```

```python
import functools
import math

import jax
import jax.numpy as jnp
import numpy as np
from jax import lax
from jax.experimental import pallas as pl
from jax.experimental.pallas import tpu as pltpu
from jax.sharding import PartitionSpec as P

EPS_SQUARED = 0.01
HIGHEST = lax.Precision.HIGHEST
MESH = pl.DeviceIdType.MESH
CHIPS_X = 4
LAG = 15
MOVE_TURN = 13
DELAY = 1
ROWS = 8
VMEM_ALL = 67043328


def spectral_tables(node_count):
    half_count = node_count // 2
    node_index = np.arange(node_count)[:, None]
    wave_index = np.arange(half_count + 1)[None, :]
    phase_angle = (node_index * wave_index % node_count) * (2.0 * math.pi / node_count)
    cosine_table = np.cos(phase_angle)
    sine_table = np.sin(phase_angle)
    wavenumber = np.arange(half_count + 1).astype(np.float64)
    inside = (wavenumber > 0) & (wavenumber < half_count)
    first_weight = np.where(inside, 2.0 * wavenumber / half_count, 0.0)
    fourth_weight = np.where(
        inside, 2.0 * (wavenumber / half_count) ** 4, np.where(wavenumber == half_count, 1.0, 0.0)
    )
    derivative = (
        (cosine_table * first_weight) @ sine_table.T - (sine_table * first_weight) @ cosine_table.T
    ) / node_count
    bending_table = (
        (cosine_table * fourth_weight) @ cosine_table.T
        + (sine_table * fourth_weight) @ sine_table.T
    ) / node_count
    return np.concatenate([derivative.T, bending_table.T], axis=1).astype(np.float32)


def iota(shape, dim):
    return lax.broadcasted_iota(jnp.int32, shape, dim)


def main_kernel(
    sizes,
    far_hbm,
    table_hbm,
    pos_hbm,
    tension_hbm,
    bending_hbm,
    order_hbm,
    dest_hbm,
    goal_hbm,
    basis_ref,
    nodes_hbm,
    force_out,
    near_out,
    split_out,
    gram_out,
    force_ref,
    near_ref,
    split_ref,
    gram_ref,
    far_ref,
    table_ref,
    pos_ref,
    tension_ref,
    bending_ref,
    order_ref,
    dest_ref,
    goal_ref,
    move_out,
    move_in,
    goal_nodes,
    speeds,
    all_basis,
    all_nodes,
    wide_nodes,
    kernels,
    part_out,
    part_in,
    line_out,
    line_in,
    sum_row,
    move_send,
    move_recv,
    node_send,
    node_recv,
    ring_send,
    ring_recv,
    first_send,
    first_recv,
    second_send,
    second_recv,
    pair_send,
    pair_recv,
    own_sem,
    part_send,
    part_recv,
    line_send,
    line_recv,
    full_send,
    full_recv,
):
    n_clu, n_col, vesicles, node_count, move_count, rank_count, source_count = sizes
    me = lax.axis_index("clu")
    z = lax.axis_index("col")
    core = lax.rem(me, 2)
    partner = me + 1 - 2 * core
    chips = min(CHIPS_X, n_clu // 2)
    members = 2 * chips
    plane = lax.div(me, members)
    across = lax.div(lax.rem(me, members), 2)
    major = across + core * (plane - across)
    minor = plane + core * (across - plane)
    lane_share = source_count // chips

    barrier = pltpu.get_barrier_semaphore()

    @pl.loop(1, n_col)
    def _(k):
        pl.semaphore_signal(
            barrier, inc=1, device_id={"col": lax.rem(z + k, n_col)}, device_id_type=MESH
        )

    @pl.loop(1, n_clu)
    def _(k):
        pl.semaphore_signal(
            barrier, inc=1, device_id={"clu": lax.rem(me + k, n_clu)}, device_id_type=MESH
        )

    loads = [
        pltpu.make_async_copy(source, place, own_sem.at[3 + at])
        for at, (source, place) in enumerate(
            (
                (pos_hbm, pos_ref),
                (table_hbm, table_ref),
                (tension_hbm, tension_ref),
                (bending_hbm, bending_ref),
                (order_hbm, order_ref),
                (dest_hbm, dest_ref),
                (goal_hbm, goal_ref),
                (far_hbm, far_ref),
            )
        )
    ]
    for load in loads:
        load.start()
    keeps = [
        pltpu.make_async_copy(source, place, own_sem.at[11 + at])
        for at, (source, place) in enumerate(
            (
                (force_ref, force_out),
                (near_ref, near_out),
                (split_ref, split_out),
                (gram_ref, gram_out),
            )
        )
    ]
    own_basis = pltpu.make_async_copy(basis_ref, all_basis.at[z], own_sem.at[0])
    own_basis.start()
    load_nodes = pltpu.make_async_copy(nodes_hbm, all_nodes.at[z], own_sem.at[1])
    load_nodes.start()
    def node_copy(k):
        return pltpu.make_async_remote_copy(
            src_ref=nodes_hbm,
            dst_ref=all_nodes.at[z],
            send_sem=node_send.at[k],
            recv_sem=node_recv.at[k],
            device_id={"col": lax.rem(z + k, n_col)},
            device_id_type=MESH,
        )

    def line_offset(turn):
        odd = lax.rem(turn, 2)
        return (1 - odd) * (lax.div(turn, 2) + 1) + odd * (n_col - lax.div(turn + 1, 2))

    def peer(down, right):
        first = lax.rem(minor + down, chips)
        second = lax.rem(major + right, chips)
        return {
            "clu": (first + core * (second - first)) * members
            + 2 * (second + core * (first - second))
            + core
        }

    def tile(ref, row, column):
        lanes = pl.ds(pl.multiple_of(column * lane_share, lane_share), lane_share)
        return ref.at[core, row, :, lanes]

    def origin_of(k):
        return lax.rem(z + n_col - k, n_col)

    def ring_copy(k):
        return pltpu.make_async_remote_copy(
            src_ref=tile(basis_ref, major, minor),
            dst_ref=tile(all_basis.at[z], major, minor),
            send_sem=ring_send.at[k],
            recv_sem=ring_recv.at[k],
            device_id={"col": lax.rem(z + k, n_col)},
            device_id_type=MESH,
        )

    def from_ring(k):
        block = tile(all_basis.at[origin_of(k)], major, minor)
        return pltpu.make_async_remote_copy(
            src_ref=block,
            dst_ref=block,
            send_sem=ring_send.at[k],
            recv_sem=ring_recv.at[k],
            device_id={"col": origin_of(k)},
            device_id_type=MESH,
        )

    def first_copy(k, d, back):
        column = lax.rem(minor + back * (chips - d), chips)
        block = tile(all_basis.at[origin_of(k)], major, column)
        return pltpu.make_async_remote_copy(
            src_ref=block,
            dst_ref=block,
            send_sem=first_send.at[k, d],
            recv_sem=first_recv.at[k, d],
            device_id=peer(chips - d if back else d, 0),
            device_id_type=MESH,
        )

    def second_copy(k, d, back):
        row = lax.rem(major + back * (chips - d), chips)
        block = all_basis.at[origin_of(k), core, row]
        return pltpu.make_async_remote_copy(
            src_ref=block,
            dst_ref=block,
            send_sem=second_send.at[k, d],
            recv_sem=second_recv.at[k, d],
            device_id=peer(0, chips - d if back else d),
            device_id_type=MESH,
        )

    def pair_copy(k, half):
        block = all_basis.at[origin_of(k), half]
        return pltpu.make_async_remote_copy(
            src_ref=block,
            dst_ref=block,
            send_sem=pair_send.at[k],
            recv_sem=pair_recv.at[k],
            device_id={"clu": partner},
            device_id_type=MESH,
        )

    def service(turn):
        @pl.when(turn < n_col - 1)
        def _():
            k = line_offset(turn)
            from_ring(k).wait_recv()
            for d in range(1, chips):
                first_copy(k, d, 0).start()

        @pl.when((turn >= LAG) & (turn < n_col - 1 + LAG))
        def _():
            k = line_offset(turn - LAG)
            for d in range(1, chips):
                first_copy(k, d, 1).wait_recv()
            for d in range(1, chips):
                second_copy(k, d, 0).start()

        @pl.when(turn >= 2 * LAG)
        def _():
            k = line_offset(turn - 2 * LAG)
            for d in range(1, chips):
                second_copy(k, d, 1).wait_recv()
            pair_copy(k, core).start()

    def move_copy(k):
        other = lax.rem(me + k, n_clu)
        return pltpu.make_async_remote_copy(
            src_ref=move_out.at[other],
            dst_ref=move_in.at[me],
            send_sem=move_send.at[k],
            recv_sem=move_recv.at[k],
            device_id={"clu": other},
            device_id_type=MESH,
        )

    def from_peer(buffer, sems_out, sems_in, axis, k, count, index):
        other = lax.rem(index + count - k, count)
        return pltpu.make_async_remote_copy(
            src_ref=buffer.at[other],
            dst_ref=buffer.at[other],
            send_sem=sems_out.at[k],
            recv_sem=sems_in.at[k],
            device_id={axis: other},
            device_id_type=MESH,
        )

    pl.semaphore_wait(barrier, n_clu + n_col - 2)

    @pl.loop(1, n_col)
    def _(k):
        node_copy(k).start()

    @pl.loop(0, n_col - 1)
    def _(turn):
        ring_copy(line_offset(turn)).start()

    for load in loads:
        load.wait()

    rows_x = pl.ds(0, vesicles, stride=2)
    rows_y = pl.ds(1, vesicles, stride=2)
    flat = jnp.concatenate([pos_ref[rows_x, :], pos_ref[rows_y, :]], axis=0)
    table = table_ref[...]
    both = jnp.dot(flat, table, precision=HIGHEST, preferred_element_type=jnp.float32)
    slope = both[:, :node_count]
    fourth = both[:, node_count:]
    tension = tension_ref[...]
    pulled = slope * jnp.concatenate([tension, tension], axis=0)
    stretch = jnp.dot(
        pulled, table[:, :node_count], precision=HIGHEST, preferred_element_type=jnp.float32
    )
    square = (vesicles, vesicles)
    bending = jnp.sum(
        jnp.where(iota(square, 0) == iota(square, 1), bending_ref[...], 0.0), axis=1, keepdims=True
    )
    force = stretch - jnp.concatenate([bending, bending], axis=0) * fourth
    force_ref[rows_x, :] = force[:vesicles]
    force_ref[rows_y, :] = force[vesicles:]
    keeps[0].start()
    carried = jnp.concatenate([flat, force], axis=0)

    pairs = (move_count, move_count)
    dest_row = dest_ref[...].astype(jnp.float32)
    dest_col = jnp.sum(
        jnp.where(iota(pairs, 0) == iota(pairs, 1), dest_row, 0.0), axis=1, keepdims=True
    )
    earlier = jnp.sum(
        jnp.where((dest_col == dest_row) & (iota(pairs, 0) < iota(pairs, 1)), 1.0, 0.0),
        axis=0,
        keepdims=True,
    )
    slot_rows = n_clu * 8
    wide = (slot_rows, move_count)
    match = (dest_row == (iota(wide, 0) // 8).astype(jnp.float32)) & (
        earlier == (iota(wide, 0) // 4 % 2).astype(jnp.float32)
    )
    order_row = order_ref[:, :move_count].astype(jnp.float32)
    goal_row = goal_ref[...].astype(jnp.float32) + 1.0
    found = jnp.sum(jnp.where(match, 1.0, 0.0), axis=1, keepdims=True)
    chosen = jnp.sum(jnp.where(match, order_row, 0.0), axis=1, keepdims=True)
    goal = jnp.sum(jnp.where(match, goal_row, 0.0), axis=1, keepdims=True)
    table_shape = (slot_rows, 4 * vesicles)
    part_first = (iota(table_shape, 0) % 4 * vesicles).astype(jnp.float32)
    lane = iota(table_shape, 1).astype(jnp.float32)
    pack = jnp.where((lane == part_first + chosen) & (found > 0.0), 1.0, 0.0)
    packed = jnp.dot(pack, carried, precision=HIGHEST, preferred_element_type=jnp.float32)
    move_out[:, 0] = packed.reshape(n_clu, 8, node_count)
    move_out[:, 1] = jnp.broadcast_to(goal, (slot_rows, node_count)).reshape(n_clu, 8, node_count)

    services = n_col - 1 + 2 * LAG
    early = n_col - 1 - DELAY
    chunk = 128
    parts = source_count // chunk

    def widen(origin):
        nodes = all_nodes[origin].astype(jnp.float32)
        for part in range(parts):
            piece = nodes[:, part * chunk : (part + 1) * chunk]
            turned = jnp.concatenate([piece] * 4, axis=0).T
            rows = slice(part * chunk, (part + 1) * chunk)
            wide_nodes[origin, rows, :node_count] = jnp.broadcast_to(
                turned[:, 0:1], (chunk, node_count)
            )
            wide_nodes[origin, rows, node_count:] = jnp.broadcast_to(
                turned[:, 1:2], (chunk, node_count)
            )

    load_nodes.wait()
    widen(z)

    def both_sides(turn, count):
        for at in range(count):
            k = line_offset(turn + at)
            from_peer(all_nodes, node_send, node_recv, "col", k, n_col, z).wait_recv()
        for at in range(count):
            widen(origin_of(line_offset(turn + at)))
        for at in range(count):

            @pl.when(turn + at >= DELAY)
            def _():
                service(turn + at - DELAY)

    @pl.loop(0, n_col // 2 - 1)
    def _(turn):
        both_sides(2 * turn, 2)

    both_sides(n_col - 2, 1)

    def form_kernel(b):
        own = far_ref[0, b]
        target_x = pos_ref[pl.ds(2 * b, 1), :]
        target_y = pos_ref[pl.ds(2 * b + 1, 1), :]
        for part in range(parts):
            rows = slice(part * chunk, (part + 1) * chunk)
            delta_x = target_x - wide_nodes[own, rows, :node_count]
            delta_y = target_y - wide_nodes[own, rows, node_count:]
            square_x = delta_x * delta_x
            square_y = delta_y * delta_y
            spread = square_x + square_y + EPS_SQUARED
            log_part = -0.5 * jnp.log(spread)
            inverse = 1.0 / spread
            kernels[b, rows, 0:node_count] = (log_part + square_x * inverse).astype(jnp.bfloat16)
            kernels[b, rows, node_count : 2 * node_count] = (
                delta_x * delta_y * inverse
            ).astype(jnp.bfloat16)
            kernels[b, rows, 2 * node_count : 3 * node_count] = (
                log_part + square_y * inverse
            ).astype(jnp.bfloat16)

    own_move = pltpu.make_async_copy(move_out.at[me], move_in.at[me], own_sem.at[2])
    own_move.start()
    begun = early
    rounds = vesicles // 2
    within = min(2 * rounds, services - begun)

    @pl.loop(0, rounds)
    def _(turn):
        form_kernel(2 * turn)

        @pl.when(2 * turn < within)
        def _():
            service(begun + 2 * turn)

        form_kernel(2 * turn + 1)

        @pl.when(2 * turn + 1 < within)
        def _():
            service(begun + 2 * turn + 1)

        @pl.when(turn == min(MOVE_TURN, rounds - 1))
        def _():
            @pl.loop(1, n_clu)
            def _(k):
                move_copy(k).start()

    @pl.loop(begun + within, services)
    def _(index):
        service(index)

    own_basis.wait()

    @pl.loop(1, n_col)
    def _(k):
        pair_copy(k, 1 - core).wait_recv()

    width = 2 * node_count

    def sketch_row(b):
        basis = all_basis[far_ref[0, b]].reshape(2 * rank_count, source_count)
        product = jnp.dot(basis, kernels[b], preferred_element_type=jnp.float32)
        row = product[:rank_count, :width] + product[rank_count:, node_count:]
        high = row.astype(jnp.bfloat16)
        lanes = pl.ds(pl.multiple_of(b * width, width), width)
        split_ref[:rank_count, lanes] = high
        split_ref[rank_count:, lanes] = (row - high.astype(jnp.float32)).astype(jnp.bfloat16)

    @pl.loop(0, vesicles // ROWS)
    def _(turn):
        for at in range(ROWS):
            sketch_row(turn * ROWS + at)

    keeps[2].start()
    split = split_ref[...]
    total = lax.dot_general(
        split, split, (((1,), (1,)), ((), ())), preferred_element_type=jnp.float32
    )
    gram = (
        total[:rank_count, :rank_count]
        + total[:rank_count, rank_count:]
        + total[rank_count:, :rank_count]
        + total[rank_count:, rank_count:]
    )
    half = rank_count // 2
    folded = jnp.concatenate([gram[:half], gram[half:]], axis=1)
    own_rows = half // n_clu
    for row in range(half):
        part_out[row // own_rows, row % own_rows : row % own_rows + 1, :] = folded[row : row + 1]

    def part_copy(k):
        other = lax.rem(me + k, n_clu)
        return pltpu.make_async_remote_copy(
            src_ref=part_out.at[other],
            dst_ref=part_in.at[me],
            send_sem=part_send.at[k],
            recv_sem=part_recv.at[k],
            device_id={"clu": other},
            device_id_type=MESH,
        )

    @pl.loop(1, n_clu)
    def _(k):
        part_copy(k).start()

    own_move.wait()

    @pl.loop(1, n_clu)
    def _(k):
        from_peer(move_in, move_send, move_recv, "clu", k, n_clu, me).wait_recv()

    goals = move_in[:, 1].reshape(slot_rows, node_count)
    goal_shape = (slot_rows, 2 * vesicles)
    part_index = iota(goal_shape, 0) % 4
    goal_lane = iota(goal_shape, 1).astype(jnp.float32)
    goal_value = goals[:, : 2 * vesicles]
    goal_hot = jnp.where(
        (goal_lane == (part_index * vesicles - 1).astype(jnp.float32) + goal_value)
        & (part_index < 2)
        & (goal_value > 0.0),
        1.0,
        0.0,
    )
    goal_nodes[...] = jnp.dot(
        goal_hot, flat, precision=HIGHEST, preferred_element_type=jnp.float32
    ).reshape(n_clu, 8, node_count)

    def near_pair(src):
        turned = move_in[src, 0].T
        goal_tile = goal_nodes[src]
        results = []
        for slot in range(2):
            first = 4 * slot
            delta_x = goal_tile[first : first + 1] - turned[:, first : first + 1]
            delta_y = goal_tile[first + 1 : first + 2] - turned[:, first + 1 : first + 2]
            push_x = turned[:, first + 2 : first + 3]
            push_y = turned[:, first + 3 : first + 4]
            spread = delta_x * delta_x + delta_y * delta_y + EPS_SQUARED
            log_part = -0.5 * jnp.log(spread)
            along = (delta_x * push_x + delta_y * push_y) * (1.0 / spread)
            results.append(jnp.sum(log_part * push_x + delta_x * along, axis=0, keepdims=True))
            results.append(jnp.sum(log_part * push_y + delta_y * along, axis=0, keepdims=True))
            results.append(jnp.zeros((2, node_count), jnp.float32))
        speeds[src] = jnp.concatenate(results, axis=0)

    @pl.loop(0, n_clu // 4)
    def _(turn):
        near_pair(2 * turn)
        near_pair(2 * turn + 1)

    part_in[me] = part_out[me]

    @pl.loop(1, n_clu)
    def _(k):
        from_peer(part_in, part_send, part_recv, "clu", k, n_clu, me).wait_recv()

    line_out[...] = jnp.sum(part_in[...], axis=0)

    def line_copy(k):
        return pltpu.make_async_remote_copy(
            src_ref=line_out,
            dst_ref=line_in.at[z],
            send_sem=line_send.at[k],
            recv_sem=line_recv.at[k],
            device_id={"col": lax.rem(z + k, n_col)},
            device_id_type=MESH,
        )

    @pl.loop(1, n_col)
    def _(k):
        line_copy(k).start()

    @pl.loop(n_clu // 4, n_clu // 2)
    def _(turn):
        near_pair(2 * turn)
        near_pair(2 * turn + 1)

    near = lax.dot_general(
        goal_hot,
        speeds[...].reshape(slot_rows, node_count),
        (((0,), (0,)), ((), ())),
        precision=HIGHEST,
        preferred_element_type=jnp.float32,
    ) * (1.0 / node_count)
    near_ref[rows_x, :] = near[:vesicles]
    near_ref[rows_y, :] = near[vesicles:]
    keeps[1].start()
    line_in[z] = line_out[...]

    @pl.loop(1, n_col)
    def _(k):
        from_peer(line_in, line_send, line_recv, "col", k, n_col, z).wait_recv()

    sum_row[...] = jnp.sum(line_in[...], axis=0)

    def full_copy(k):
        return pltpu.make_async_remote_copy(
            src_ref=sum_row,
            dst_ref=gram_ref.at[me],
            send_sem=full_send.at[k],
            recv_sem=full_recv.at[k],
            device_id={"clu": lax.rem(me + k, n_clu)},
            device_id_type=MESH,
        )

    @pl.loop(1, n_clu)
    def _(k):
        full_copy(k).start()

    gram_ref[me] = sum_row[...]

    @pl.loop(1, n_col)
    def _(k):
        node_copy(k).wait_send()
        line_copy(k).wait_send()
        pair_copy(k, core).wait_send()
        ring_copy(k).wait_send()
        for d in range(1, chips):
            first_copy(k, d, 0).wait_send()
            second_copy(k, d, 0).wait_send()

    @pl.loop(1, n_clu)
    def _(k):
        move_copy(k).wait_send()
        part_copy(k).wait_send()

    @pl.loop(1, n_clu)
    def _(k):
        full_copy(k).wait_send()
        from_peer(gram_ref, full_send, full_recv, "clu", k, n_clu, me).wait_recv()

    keeps[3].start()
    for keep in keeps:
        keep.wait()


def lower_inverse(gram):
    rank_count = gram.shape[0]
    square = (rank_count, rank_count)
    eye = jnp.where(iota(square, 0) == iota(square, 1), 1.0, 0.0)
    joined = jnp.concatenate([gram, eye], axis=1)
    width = 2 * rank_count
    count = rank_count // 8
    tiles = [joined[8 * t : 8 * t + 8] for t in range(count)]
    row_of = iota((8, width), 0)
    for first in range(0, rank_count, 4):
        home, spot = divmod(first, 8)
        tile = tiles[home]
        rows = [tile[spot + i : spot + i + 1] for i in range(4)]
        pivot = [
            [
                jnp.broadcast_to(rows[i][:, first + k : first + k + 1], (1, width))
                for k in range(4)
            ]
            for i in range(4)
        ]
        columns = {
            t: [
                jnp.broadcast_to(tiles[t][:, first + k : first + k + 1], (8, width))
                for k in range(4)
            ]
            for t in range(home, count)
        }
        inverses = []
        for i in range(4):
            inverses.append(1.0 / pivot[i][i])
            for m in range(i + 1, 4):
                ratio = pivot[i][m] * inverses[i]
                rows[m] = rows[m] - ratio * rows[i]
                for k in range(m, 4):
                    pivot[m][k] = pivot[m][k] - ratio * pivot[i][k]
        for t in range(home, count):
            factors = []
            for i in range(4):
                value = columns[t][i]
                for q in range(i):
                    value = value - factors[q] * pivot[q][i]
                factors.append(value * inverses[i])
            updated = tiles[t] - (
                (factors[0] * rows[0] + factors[1] * rows[1])
                + (factors[2] * rows[2] + factors[3] * rows[3])
            )
            if t == home:
                updated = jnp.where(row_of > spot + 3, updated, tile)
                for i in range(1, 4):
                    updated = jnp.where(row_of == spot + i, rows[i], updated)
            tiles[t] = updated
    whole = jnp.concatenate(tiles, axis=0)
    pivots = jnp.sum(whole[:, :rank_count] * eye, axis=1, keepdims=True)
    return whole[:, rank_count:] / jnp.sqrt(pivots)


def finish_kernel(
    scale_factor,
    gram_in,
    split_in,
    force_in,
    near_in,
    basis_out,
    force_out,
    near_out,
    gram_ref,
    split_ref,
    force_ref,
    near_ref,
    spread_ref,
    staged,
    sems,
):
    vesicles, rows, node_count = staged.shape
    rank_count = rows // 2
    loads = [
        pltpu.make_async_copy(source, place, sems.at[2 + at])
        for at, (source, place) in enumerate(
            (
                (gram_in, gram_ref),
                (force_in, force_ref),
                (near_in, near_ref),
                (split_in, split_ref),
            )
        )
    ]
    for load in loads:
        load.start()
    loads[0].wait()
    folded = gram_ref[...]
    gram = jnp.concatenate([folded[:, :rank_count], folded[:, rank_count:]], axis=0)
    lower = lower_inverse(gram) * scale_factor
    for load in loads[1:]:
        load.wait()
    send_force = pltpu.make_async_copy(force_ref, force_out, sems.at[0])
    send_near = pltpu.make_async_copy(near_ref, near_out, sems.at[1])
    send_force.start()
    send_near.start()
    zeros = jnp.zeros_like(lower)
    spread_ref[pl.ds(0, rank_count, stride=2), :] = jnp.concatenate([lower, zeros], axis=1)
    spread_ref[pl.ds(1, rank_count, stride=2), :] = jnp.concatenate([zeros, lower], axis=1)
    spread = spread_ref[...]
    high = spread.astype(jnp.bfloat16)
    low = (spread - high.astype(jnp.float32)).astype(jnp.bfloat16)
    factors = jnp.concatenate([high, low, high, low], axis=1)
    group = 4
    sends = []
    for first in range(0, vesicles, group):
        for b in range(first, first + group):
            lanes = slice(2 * b * node_count, (2 * b + 1) * node_count)
            others = slice((2 * b + 1) * node_count, (2 * b + 2) * node_count)
            upper = [split_ref[:rank_count, lanes], split_ref[:rank_count, others]]
            under = [split_ref[rank_count:, lanes], split_ref[rank_count:, others]]
            staged[b] = jnp.dot(
                factors,
                jnp.concatenate(upper + upper + under + under, axis=0),
                preferred_element_type=jnp.float32,
            )
        rows_now = pl.ds(first, group)
        send = pltpu.make_async_copy(
            staged.at[rows_now], basis_out.at[rows_now], sems.at[6 + first // group]
        )
        send.start()
        sends.append(send)
    for send in sends:
        send.wait()
    send_force.wait()
    send_near.wait()


def per_device(
    positions,
    tension,
    bending,
    moved_order,
    move_destination,
    move_target,
    far_range,
    old_basis,
    source_nodes,
):
    n_clu, n_col = lax.axis_size("clu"), lax.axis_size("col")
    vesicles, node_count = positions.shape[0], positions.shape[2]
    move_count = move_target.shape[0]
    rank_count, source_count = old_basis.shape[0] // 2, old_basis.shape[1]
    half = rank_count // 2
    own_rows = half // n_clu
    chips = min(CHIPS_X, n_clu // 2)
    row_share = rank_count // chips
    f32, bf16, i32 = jnp.float32, jnp.bfloat16, jnp.int32
    vmem, dma = pltpu.VMEM, pltpu.SemaphoreType.DMA
    in_hbm = pl.BlockSpec(memory_space=pltpu.HBM)
    sizes = (n_clu, n_col, vesicles, node_count, move_count, rank_count, source_count)
    flat_shape = jax.ShapeDtypeStruct((2 * vesicles, node_count), f32)
    force, near, split, gram = pl.pallas_call(
        functools.partial(main_kernel, sizes),
        out_shape=(
            flat_shape,
            flat_shape,
            jax.ShapeDtypeStruct((2 * rank_count, vesicles * 2 * node_count), bf16),
            jax.ShapeDtypeStruct((n_clu, own_rows, 2 * rank_count), f32),
        ),
        in_specs=[in_hbm] * 10,
        out_specs=[in_hbm] * 4,
        scratch_shapes=[
            vmem((2 * vesicles, node_count), f32),
            vmem((2 * vesicles, node_count), f32),
            vmem((2 * rank_count, vesicles * 2 * node_count), bf16),
            vmem((n_clu, own_rows, 2 * rank_count), f32),
            pltpu.SMEM((1, vesicles), i32),
            vmem((node_count, 2 * node_count), f32),
            vmem((2 * vesicles, node_count), f32),
            vmem((vesicles, node_count), f32),
            vmem((1, vesicles), f32),
            vmem((1, vesicles), i32),
            vmem((1, move_count), i32),
            vmem((1, move_count), i32),
            vmem((n_clu, 2, 8, node_count), f32),
            vmem((n_clu, 2, 8, node_count), f32),
            vmem((n_clu, 8, node_count), f32),
            vmem((n_clu, 8, node_count), f32),
            vmem((n_col, 2, chips, row_share, source_count), bf16),
            vmem((n_col, 2, source_count), bf16),
            vmem((n_col, source_count, 2 * node_count), f32),
            vmem((vesicles, source_count, 3 * node_count), bf16),
            vmem((n_clu, own_rows, 2 * rank_count), f32),
            vmem((n_clu, own_rows, 2 * rank_count), f32),
            vmem((own_rows, 2 * rank_count), f32),
            vmem((n_col, own_rows, 2 * rank_count), f32),
            vmem((own_rows, 2 * rank_count), f32),
            dma((n_clu,)),
            dma((n_clu,)),
            dma((n_col,)),
            dma((n_col,)),
            dma((n_col,)),
            dma((n_col,)),
            dma((n_col, chips)),
            dma((n_col, chips)),
            dma((n_col, chips)),
            dma((n_col, chips)),
            dma((n_col,)),
            dma((n_col,)),
            dma((15,)),
            dma((n_clu,)),
            dma((n_clu,)),
            dma((n_col,)),
            dma((n_col,)),
            dma((n_clu,)),
            dma((n_clu,)),
        ],
        compiler_params=pltpu.CompilerParams(
            collective_id=0, has_side_effects=True, vmem_limit_bytes=VMEM_ALL
        ),
        name="main_step",
    )(
        far_range.reshape(1, vesicles),
        jnp.asarray(spectral_tables(node_count)),
        positions.reshape(2 * vesicles, node_count),
        tension,
        bending.reshape(1, vesicles),
        moved_order,
        move_destination.reshape(1, move_count),
        move_target.reshape(1, move_count),
        old_basis.reshape(2, chips, row_share, source_count),
        source_nodes,
    )
    scale_factor = math.sqrt(2.0 * node_count * vesicles * n_clu * n_col)
    new_basis, force, near = pl.pallas_call(
        functools.partial(finish_kernel, scale_factor),
        out_shape=(
            jax.ShapeDtypeStruct((vesicles, 2 * rank_count, node_count), f32),
            flat_shape,
            flat_shape,
        ),
        in_specs=[in_hbm] * 4,
        out_specs=[in_hbm] * 3,
        scratch_shapes=[
            vmem((half, 2 * rank_count), f32),
            vmem((2 * rank_count, vesicles * 2 * node_count), bf16),
            vmem((2 * vesicles, node_count), f32),
            vmem((2 * vesicles, node_count), f32),
            vmem((2 * rank_count, 2 * rank_count), f32),
            vmem((vesicles, 2 * rank_count, node_count), f32),
            dma((6 + vesicles // 4,)),
        ],
        compiler_params=pltpu.CompilerParams(vmem_limit_bytes=VMEM_ALL),
        name="finish_step",
    )(gram.reshape(half, 2 * rank_count), split, force, near)
    return (
        force.reshape(vesicles, 2, node_count),
        near.reshape(vesicles, 2, node_count),
        new_basis.reshape(vesicles, rank_count, 2, node_count),
    )


def solution(mesh):
    placed = (
        P(("clu", "col"), None, None),
        P(("clu", "col"), None),
        P(("clu", "col")),
        P(("clu", "col"), None),
        P(("clu", "col"), None),
        P(("clu", "col")),
        P(("clu", "col"), None),
        P(None, "col"),
        P(None, "col"),
    )
    return jax.shard_map(
        per_device,
        mesh=mesh,
        in_specs=placed,
        out_specs=(
            P(("clu", "col"), None, None),
            P(("clu", "col"), None, None),
            P(("clu", "col"), None, None, None),
        ),
        check_vma=False,
    )
```
